32 devices in a mesh: traj: 2 (over y), ctx: 8 (over z, x), head: 2 (over core).
Axes of the slice: x: 2, y: 2, z: 4, core: 2. Of those that a mesh axis runs over, the one named last changes fastest.
Arguments:
- features: bfloat16 [4096, 2048], P(('traj', 'ctx'), 'head'), parts along dimension 0, may hold values from -6 to 6
- b_input: bfloat16 [4096, 128], P(('traj', 'ctx')), parts along dimension 0, may hold values from -1.5 to 1.5
- c_input: bfloat16 [4096, 128], P(('traj', 'ctx')), parts along dimension 0, may hold values from -1.5 to 1.5
- step_input: float32 [64, 4096], P('head', ('traj', 'ctx')), parts along dimension 1, may hold values from -5.5 to 18.78016
- decay_log: float32 [64], P('head')
- skip_gain: float32 [64], P('head'), may hold values from 0.5 to 2
- norm_gain: float32 [2048], P('head'), may hold values from 0.25 to 1.75
- value_weight: float32 [2048], P('head'), may hold values from -0.125 to 0.125
- rewards: float32 [4096], P(('traj', 'ctx')), parts along dimension 0, may hold values from -0.3 to 0.3
- reward_keep_mask: int32 [4096], P(('traj', 'ctx')), parts along dimension 0, may hold values 0 or 1
- episode_end: int32 [4096], P(('traj', 'ctx')), parts along dimension 0, may hold values from 0 to 1
Outputs:
- values: float32 [4096], P(('traj', 'ctx')), parts along dimension 0
- advantages: float32 [4096], P(('traj', 'ctx')), parts along dimension 0
The draws below stay inside these ranges and needn't reach their ends.
There are 2 independent parts, one for each index of `traj`. The reference program is written for one: setup_inputs(seed, part) draws one part's arguments, and reference() takes and returns one part's arrays. A program takes and returns all parts, laid end to end along the dimension named above; an argument that names none is the same for every part. Nothing has to cross between parts.
All inputs are finite; a program needn't handle non-finite values. No bound on the sum of `reward_keep_mask` on one device may be relied on, other than what follows from the above.
Results may differ from the reference program's by a relative error of at most 0.00037.
Values sent between devices are 32-bit elements; how exact they have to be, the bound alone decides.
A program may use at most 192 MiB of HBM per device.

```python
import jax
import jax.numpy as jnp
from jax import lax

HEADS = 64
HEAD_DIM = 32
STATE = 128
SPAN = 256
TOK_DEV = 256
TRAJECTORY_TOKENS = 2048


def cluster_matches(key):
    cluster_locations = jax.random.randint(jax.random.fold_in(key, 4242), (2,), 0, TRAJECTORY_TOKENS)
    return jnp.any(jnp.arange(TRAJECTORY_TOKENS)[:, None] == cluster_locations[None, :], axis=1)


def draw_b_input(key, part):
    matched_entries = cluster_matches(key)
    baseline_values = 0.25 * jax.random.normal(jax.random.fold_in(key, 11), (TRAJECTORY_TOKENS, STATE), jnp.float32)
    baseline_values = jnp.clip(baseline_values, -1.5, 1.5)
    cluster_length = 0.00917 * TRAJECTORY_TOKENS
    return jnp.where(matched_entries[:, None], baseline_values / cluster_length, baseline_values).astype(jnp.bfloat16)


def draw_step_input(key, part):
    matched_entries = cluster_matches(key)
    uniform_part = jax.random.uniform(jax.random.fold_in(key, 21), (HEADS, TRAJECTORY_TOKENS), jnp.float32)
    baseline_values = -5.5 + 0.3 * uniform_part
    cluster_length = 0.00917 * TRAJECTORY_TOKENS
    return jnp.where(matched_entries[None, :], cluster_length, baseline_values)


def draw_decay_log(key, part):
    mean_step = 0.0131
    picker = jax.random.uniform(jax.random.fold_in(key, 31), (HEADS,), jnp.float32)
    slow_factor = jnp.exp(jax.random.uniform(jax.random.fold_in(key, 32), (HEADS,), jnp.float32, jnp.log(0.5), jnp.log(1.2)))
    middle_factor = jnp.exp(jax.random.uniform(jax.random.fold_in(key, 33), (HEADS,), jnp.float32, 0.0, jnp.log(3.0)))
    fast_factor = jnp.exp(jax.random.uniform(jax.random.fold_in(key, 34), (HEADS,), jnp.float32, jnp.log(0.02), jnp.log(0.08)))
    slow_rate = slow_factor * 0.6931 / (TRAJECTORY_TOKENS * mean_step)
    middle_rate = middle_factor / (TOK_DEV * mean_step)
    fast_rate = fast_factor / mean_step
    rate = jnp.where(picker < 0.5, slow_rate, jnp.where(picker < 0.75, middle_rate, fast_rate))
    return jnp.log(rate)


def draw_episode_end(key, part):
    silent_length = TRAJECTORY_TOKENS * 5 // 8
    silent_start = jax.random.randint(jax.random.fold_in(key, 51), (), 0, TRAJECTORY_TOKENS - silent_length + 1).astype(jnp.int32)
    position = jnp.arange(TRAJECTORY_TOKENS).astype(jnp.int32)
    sparse_ends = jax.random.randint(jax.random.fold_in(key, 52), (TRAJECTORY_TOKENS,), 0, TOK_DEV * 4) == 0
    silent_span = (position >= silent_start) & (position < silent_start + silent_length)
    planted = (position == silent_start - 1) | (position == silent_start + silent_length - 1)
    return jnp.where(sparse_ends & jnp.logical_not(silent_span) | planted, 1, 0).astype(jnp.int32)


def plant(values, own_key, low, largest):
    dims = values.shape
    index_at = [jax.random.randint(jax.random.fold_in(own_key, axis), (), 0, dims[axis]) for axis in range(len(dims))]
    values = values.at[tuple(index_at)].set(low)
    longest = dims.index(max(dims))
    index_at[longest] = (index_at[longest] + 1) % dims[longest]
    return values.at[tuple(index_at)].set(largest)


def levels(own_key, extent, cuts, low, top_value):
    loudness, own = 1.0, jax.random.fold_in(own_key, 6)
    for dim, blocks in cuts:
        steps = jnp.exp(jax.random.uniform(jax.random.fold_in(own, dim), (blocks,), jnp.float32, low / len(cuts), top_value / len(cuts)))
        loudness = loudness * jnp.repeat(steps, extent[dim] // blocks).reshape([-1 if axis == dim else 1 for axis in range(len(extent))])
    return loudness


def gaussian(own_key, dims, scale, limit, split=(), kind=jnp.bfloat16):
    values = jax.random.normal(own_key, dims, jnp.float32) * scale
    if len(split) > 0:
        values = levels(own_key, dims, split, -0.22, 0.18) * values
    return jnp.clip(values, min=-limit, max=limit).astype(kind)


def setup_inputs(seed: int = 0, part: int = 0) -> dict:
    arg_keys = jax.random.split(jax.random.key(seed), 12)
    part_splits = jax.random.split(jax.random.fold_in(arg_keys[11], part), 12)
    features = gaussian(part_splits[0], (TRAJECTORY_TOKENS, HEADS * HEAD_DIM), 1.0, 6.0, ((0, 8), (1, 2)))
    b_input = draw_b_input(jax.random.fold_in(jax.random.fold_in(arg_keys[11], part), 71), part)
    c_input = gaussian(part_splits[2], (TRAJECTORY_TOKENS, STATE), 0.25, 1.5, ((0, 8),))
    step_input = draw_step_input(jax.random.fold_in(jax.random.fold_in(arg_keys[11], part), 71), part)
    decay_log = draw_decay_log(jax.random.fold_in(arg_keys[11], 71), part)
    skip_gain = jnp.clip(0.5 + 1.5 * jax.random.uniform(arg_keys[5], (HEADS,), jnp.float32) ** levels(arg_keys[5], (HEADS,), ((0, 2),), -0.2, 0.2), 0.5, 2.0)
    norm_gain = jnp.clip(1.0 + 0.15 * jax.random.normal(arg_keys[6], (HEADS * HEAD_DIM,), jnp.float32), 0.25, 1.75)
    value_weight = gaussian(arg_keys[7], (HEADS * HEAD_DIM,), (HEADS * HEAD_DIM) ** -0.5, 0.125, ((0, 2),), jnp.float32)
    rewards = gaussian(part_splits[8], (TRAJECTORY_TOKENS,), 0.05, 0.3, ((0, 8),), jnp.float32)
    reward_keep_mask = plant((jax.random.randint(part_splits[9], (TRAJECTORY_TOKENS,), 0, 2) < 1).astype(jnp.int32), jax.random.fold_in(part_splits[9], 1), 0, 1)
    episode_end = draw_episode_end(jax.random.fold_in(jax.random.fold_in(arg_keys[11], part), 71), part)
    return {"features": features, "b_input": b_input, "c_input": c_input, "step_input": step_input, "decay_log": decay_log, "skip_gain": skip_gain, "norm_gain": norm_gain, "value_weight": value_weight, "rewards": rewards, "reward_keep_mask": reward_keep_mask, "episode_end": episode_end}


NORM_EPSILON = 1e-05
FULL_PRECISION = lax.Precision.HIGHEST

def reference(features, b_input, c_input, step_input, decay_log, skip_gain, norm_gain, value_weight, rewards, reward_keep_mask, episode_end):
    span_count = TRAJECTORY_TOKENS // SPAN
    row_width = HEADS * HEAD_DIM
    step_size = jax.nn.softplus(step_input)
    log_decay = (-jnp.exp(decay_log))[:, None] * step_size
    cumulative = jnp.cumsum(log_decay.reshape(HEADS, span_count, SPAN), axis=2)
    step_spans = step_size.reshape(HEADS, span_count, SPAN)
    readout = value_weight * norm_gain
    causal = jnp.arange(SPAN)[:, None] >= jnp.arange(SPAN)[None, :]

    def one_block(state, block):
        feat_block, key_block, query_block, cum_block, step_block = block
        feat_wide = feat_block.reshape(SPAN, HEADS, HEAD_DIM).astype(jnp.float32)
        scores = jnp.dot(query_block, key_block.T, preferred_element_type=jnp.float32)
        log_gap = jnp.where(causal[None], cum_block[:, :, None] - cum_block[:, None, :], 0.0)
        weights = jnp.where(causal[None], scores[None] * jnp.exp(log_gap) * step_block[:, None, :], 0.0)
        weights = lax.optimization_barrier(weights.astype(jnp.bfloat16)).astype(jnp.float32)
        intra = jnp.einsum('hts,shp->thp', weights, feat_wide, precision=FULL_PRECISION)
        carried = jnp.einsum('tn,hpn->thp', query_block.astype(jnp.float32), state, precision=FULL_PRECISION)
        carried = carried * jnp.exp(cum_block).T[:, :, None]
        block_total = cum_block[:, -1]
        coefficient = (jnp.exp(block_total[:, None] - cum_block) * step_block).T
        scaled = coefficient[:, :, None] * feat_wide
        scaled = lax.optimization_barrier(scaled.astype(jnp.bfloat16)).astype(jnp.float32)
        block_state = jnp.einsum('shp,sn->hpn', scaled, key_block.astype(jnp.float32), precision=FULL_PRECISION)
        new_state = jnp.exp(block_total)[:, None, None] * state + block_state
        mixed = (intra + carried + skip_gain[None, :, None] * feat_wide).reshape(SPAN, row_width)
        mean_square = lax.optimization_barrier(jnp.mean(mixed * mixed, axis=1))
        block_values = jnp.dot(mixed, readout, precision=FULL_PRECISION) / jnp.sqrt(mean_square + NORM_EPSILON)
        return (new_state, block_values)
    start_state = jnp.zeros((HEADS, HEAD_DIM, STATE), jnp.float32)
    blocks = (features.reshape(span_count, SPAN, row_width), b_input.reshape(span_count, SPAN, STATE), c_input.reshape(span_count, SPAN, STATE), jnp.transpose(cumulative, (1, 0, 2)), jnp.transpose(step_spans, (1, 0, 2)))
    final_state, value_blocks = lax.scan(one_block, start_state, blocks)
    values = value_blocks.reshape(TRAJECTORY_TOKENS)
    live_rewards = reward_keep_mask.astype(jnp.float32) * rewards
    keep_flags = 1.0 - episode_end.astype(jnp.float32)
    next_values = jnp.concatenate([values[1:], jnp.zeros((1,), jnp.float32)])
    delta = live_rewards + keep_flags * next_values - values

    def backward(carry_value, item):
        delta_here, keep_here = item
        result = delta_here + keep_here * carry_value
        return (result, result)
    final_carry, advantages = lax.scan(backward, jnp.zeros((), jnp.float32), (delta, keep_flags), reverse=True)
    return (values, advantages)
```

```python
import functools

import jax
import jax.numpy as jnp
from jax import lax
from jax.experimental import pallas as pl
from jax.experimental.pallas import tpu as pltpu
from jax.sharding import PartitionSpec as P

HEADS = 64
HEAD_DIM = 32
SPAN = 256
NORM_EPSILON = 1e-05
FULL = lax.Precision.HIGHEST
MESH = pl.DeviceIdType.MESH
F32 = jnp.float32
BF16 = jnp.bfloat16
GROUPS = 8
RANKS = 4
PARTS = GROUPS // RANKS
SPLIT = 4
ROWS = 128 // SPLIT
HEAD_ROWS = 8
MASKS = (3, 1, 2)
EARLY = 5


def thirds(x):
    hi = x.astype(BF16)
    rest = x - hi.astype(F32)
    mid = rest.astype(BF16)
    lo = (rest - mid.astype(F32)).astype(BF16)
    return hi, mid, lo


def dot(a, b):
    return jnp.dot(a, b, preferred_element_type=F32)


def row_to_column(row, size):
    eye = lax.broadcasted_iota(jnp.int32, (size, size), 0) == lax.broadcasted_iota(jnp.int32, (size, size), 1)
    return jnp.sum(jnp.where(eye, jnp.broadcast_to(row, (size, size)), 0.0), axis=1, keepdims=True)


def kernel(
    count,
    *refs,
):
    sources, (out, *scratch) = refs[:11], refs[11:]
    here, sem_in = scratch[:11], scratch[11]
    run(count, sources, sem_in, out, *here, *scratch[12:])


def run(
    count, sources, sem_in, out,
    feat, b_in, c_in, step_in, decay_log, skip, gain, weight, rewards, keep, ends,
    rows, expl, base, scores, state, square_state, passed, got_passed, enter, got_enter, read_rows,
    box, note, sums, sums_other,
    s1, r1, s2, r2, s3, r3, sn, rn, sh, rh,
):
    held_here = (feat, b_in, c_in, step_in, decay_log, skip, gain, weight, rewards, keep, ends)
    loads = [pltpu.make_async_copy(sources[i], held_here[i], sem_in.at[i]) for i in range(11)]
    for i in (3, 4, 0, 1, 2, 5, 6, 7, 8, 9, 10):
        loads[i].start()
    me = lax.axis_index("ctx")
    rank = lax.rem(me, RANKS)
    square_first = me - rank
    last_square = count - RANKS
    other_head = 1 - lax.axis_index("head")

    def peer(mask):
        return jnp.bitwise_xor(rank, mask)

    barrier = pltpu.get_barrier_semaphore()

    def greet(offset, _):
        pl.semaphore_signal(barrier, inc=1, device_id={"ctx": lax.rem(me + offset, count)}, device_id_type=MESH)
        return 0

    lax.fori_loop(1, count, greet, 0)
    pl.semaphore_signal(barrier, inc=1, device_id={"head": other_head}, device_id_type=MESH)

    row_i = lax.broadcasted_iota(jnp.int32, (SPAN, SPAN), 0)
    col_i = lax.broadcasted_iota(jnp.int32, (SPAN, SPAN), 1)
    upto = (row_i <= col_i).astype(BF16)
    pick_row = lax.broadcasted_iota(jnp.int32, (128, 512), 0)
    pick_head = lax.broadcasted_iota(jnp.int32, (128, 512), 1) // HEAD_DIM
    pick_low = jnp.where(pick_row < 96, lax.rem(pick_row, 32), -1)

    def pick(half):
        return (pick_low == pick_head + 16 * half).astype(BF16)

    loads[3].wait()
    loads[4].wait()
    step = jax.nn.softplus(step_in[...])
    log_decay = -jnp.exp(row_to_column(decay_log[...], 32)) * step
    cum_parts = dot(jnp.concatenate(thirds(log_decay), axis=0), upto)
    cum = cum_parts[0:32] + cum_parts[32:64] + cum_parts[64:96]
    total = cum[:, SPAN - 1 : SPAN]
    rows[0:32, :] = cum
    rows[32:64, :] = step
    none = jnp.zeros((32, SPAN), BF16)

    def columns_of(values):
        stacked = jnp.concatenate([*thirds(values), none], axis=0)
        return jnp.transpose(stacked.astype(F32)).astype(BF16)

    scale_cols = columns_of(jnp.exp(total - cum) * step)
    grow_cols = columns_of(jnp.exp(cum))

    loads[0].wait()
    loads[1].wait()
    keys = jnp.transpose(b_in[...].astype(F32)).astype(BF16)

    def copy(src, dst, send, recv, where):
        return pltpu.make_async_remote_copy(
            src_ref=src, dst_ref=dst, send_sem=send, recv_sem=recv, device_id=where, device_id_type=MESH
        )

    def state_rows(part):
        first = HEAD_ROWS + part * ROWS
        return pl.ds(0, HEAD_ROWS + ROWS) if part == 0 else pl.ds(first, ROWS)

    def plain_rows(part):
        return pl.ds(part * ROWS, ROWS)

    chunks = [(half, part) for half in range(PARTS) for part in range(SPLIT)]

    def gather_copy(mask, i):
        half, part = chunks[i]
        at = state_rows(part)
        return copy(
            state.at[peer(mask) + RANKS * half, at], square_state.at[rank, half, at],
            s1.at[mask - 1, i], r1.at[mask - 1, i], {"ctx": square_first + peer(mask)},
        )

    def pass_copy(i):
        half, part = chunks[i]
        at = plain_rows(part)
        return copy(
            passed.at[half, at], got_passed.at[half, at], s2.at[i], r2.at[i], {"ctx": lax.rem(me + RANKS, count)}
        )

    def enter_copy(mask, i):
        half, part = chunks[i]
        at = plain_rows(part)
        return copy(
            enter.at[peer(mask), half, at], got_enter.at[mask - 1, half, at],
            s3.at[mask - 1, i], r3.at[mask - 1, i], {"ctx": square_first + peer(mask)},
        )

    for half in range(PARTS):
        at = slice(512 * half, 512 * half + 512)
        chosen = pick(half)
        scaled = (dot(scale_cols, chosen) * feat[:, at].astype(F32)).astype(BF16)
        block_state = dot(keys, scaled)
        decay = dot(grow_cols[SPAN - 16 : SPAN], chosen)[8:16]
        for g in range(RANKS):
            lanes = slice(128 * g, 128 * g + 128)
            state[RANKS * half + g, 0:HEAD_ROWS] = decay[:, lanes]
            state[RANKS * half + g, HEAD_ROWS : HEAD_ROWS + 128] = block_state[:, lanes]
        if half == 0:
            pl.semaphore_wait(barrier, count)
        for i, (own_half, _) in enumerate(chunks):
            if own_half == half:
                for mask in MASKS:
                    gather_copy(mask, i).start()
        square_state[rank, half] = state[rank + RANKS * half]

    for half in range(PARTS):
        expl[:, 512 * half : 512 * half + 512] = dot(grow_cols, pick(half))
    for i in (2, 5, 6, 7, 8, 9, 10):
        loads[i].wait()

    live = keep[...].astype(F32) * rewards[...]
    end_row = ends[...].astype(F32)
    end_rows = jnp.broadcast_to(end_row, (8, SPAN)).astype(BF16)
    before = dot(end_rows, (row_i < col_i).astype(BF16))[0:1]
    end_total = before[:, SPAN - 1 : SPAN] + end_row[:, SPAN - 1 : SPAN]
    reach = ((row_i >= col_i) & (row_to_column(before, SPAN) == before)).astype(F32)
    local_sum = jnp.dot(
        jnp.broadcast_to(live, (8, SPAN)), reach, precision=FULL, preferred_element_type=F32
    )[0:1]
    open_row = (before == end_total).astype(F32)
    note[0:1, :] = jnp.broadcast_to(open_row[:, 0:1], (1, 128))
    note[1:2, :] = jnp.broadcast_to(local_sum[:, 0:1], (1, 128))
    note[2:8, :] = jnp.zeros((6, 128), F32)

    def tell(offset):
        return copy(note, box.at[offset], sn.at[offset], rn.at[offset], {"ctx": lax.rem(me + offset, count)})

    def tell_start(offset, _):
        tell(offset).start()
        return 0

    lax.fori_loop(1, count, tell_start, 0)

    scores[...] = lax.dot_general(c_in[...], b_in[...], (((1,), (1,)), ((), ())), preferred_element_type=F32)
    skip_cols = jnp.broadcast_to(skip[...], (8, 32))
    skip_parts = jnp.concatenate([*(one.astype(F32) for one in thirds(skip_cols)), jnp.zeros((8, 32), F32)], axis=1)
    for half in range(2):
        skip_lanes = dot(skip_parts.astype(BF16), pick(half))
        at = slice(512 * half, 512 * half + 512)
        base[:, at] = skip_lanes[0:1] * feat[:, at].astype(F32)
    causal = row_i[0:128, 0:128] >= col_i[0:128, 0:128]
    lane_head = lax.broadcasted_iota(jnp.int32, (SPAN, 128), 1) // HEAD_DIM

    def intra(unit):
        at = slice(unit * 128, unit * 128 + 128)
        aligned = unit // 2 * 8
        cum_rows = rows[aligned : 8 + aligned, :]
        step_rows = rows[32 + aligned : 40 + aligned, :]
        cum_cols = jnp.transpose(cum_rows)
        values = feat[:, at].astype(F32)
        top = base[0:128, at]
        low = base[128:256, at]
        for lane_h in range(4):
            h = lane_h + unit % 2 * 4
            masked = jnp.where(lane_head == lane_h, values, 0.0).astype(BF16)
            c_t0, c_t1 = cum_cols[0:128, h : h + 1], cum_cols[128:256, h : h + 1]
            c_s0, c_s1 = cum_rows[h : h + 1, 0:128], cum_rows[h : h + 1, 128:256]
            d_s0, d_s1 = step_rows[h : h + 1, 0:128], step_rows[h : h + 1, 128:256]
            w_tl = jnp.where(causal, scores[0:128, 0:128] * jnp.exp(c_t0 - c_s0) * d_s0, 0.0).astype(BF16)
            w_bl = (scores[128:256, 0:128] * jnp.exp(c_t1 - c_s0) * d_s0).astype(BF16)
            w_br = jnp.where(causal, scores[128:256, 128:256] * jnp.exp(c_t1 - c_s1) * d_s1, 0.0).astype(BF16)
            top = top + dot(w_tl, masked[0:128])
            low = low + dot(jnp.concatenate([w_bl, w_br], axis=1), masked)
        base[0:128, at] = top
        base[128:256, at] = low

    def rest():
        for unit in range(EARLY, GROUPS):
            intra(unit)

    for unit in range(EARLY):
        intra(unit)
    pl.when(square_first > 0)(rest)

    for i, (half, part) in enumerate(chunks):
        for mask in MASKS:
            gather_copy(mask, i).wait_recv()
        held = pl.ds(HEAD_ROWS + part * ROWS, ROWS)
        at = plain_rows(part)
        blocks = [square_state[k, half, held] for k in range(RANKS)]
        decays = [square_state[k, half, HEAD_ROWS - 1 : HEAD_ROWS] for k in range(RANKS)]

        @pl.when(square_first == 0)
        def _():
            second = blocks[0]
            third = decays[1] * second + blocks[1]
            fourth = decays[2] * third + blocks[2]
            passed[half, at] = decays[3] * fourth + blocks[3]
            pass_copy(i).start()
            enter[0, half, at] = jnp.zeros_like(second)
            enter[1, half, at] = second
            enter[2, half, at] = third
            enter[3, half, at] = fourth

        @pl.when(square_first > 0)
        def _():
            pass_copy(i).wait_recv()
            first = got_passed[half, at]
            second = decays[0] * first + blocks[0]
            third = decays[1] * second + blocks[1]
            fourth = decays[2] * third + blocks[2]

            @pl.when(square_first < last_square)
            def _():
                passed[half, at] = decays[3] * fourth + blocks[3]
                pass_copy(i).start()

            enter[0, half, at] = first
            enter[1, half, at] = second
            enter[2, half, at] = third
            enter[3, half, at] = fourth

        for mask in MASKS:
            enter_copy(mask, i).start()

    pl.when(square_first == 0)(rest)

    queries = c_in[...]
    readout = weight[...] * gain[...]
    sums[...] = jnp.zeros((8, SPAN), F32)
    for g in range(GROUPS):
        read_rows[g : g + 1, :] = readout[:, 128 * g : 128 * g + 128]

    def read(entering, group, held):
        square, linear = held
        hi, mid, _ = thirds(entering)
        carried = dot(queries, hi) + dot(queries, mid)
        at = pl.ds(pl.multiple_of(group * 128, 128), 128)
        mixed = base[:, at] + expl[:, at] * carried
        return square + mixed * mixed, linear + mixed * read_rows[pl.ds(group, 1), :]

    zero = jnp.zeros((SPAN, 128), F32)
    held = (zero, zero)
    for half in range(PARTS):
        held = read(enter[rank, half], rank + RANKS * half, held)
    for half in range(PARTS):
        for mask in MASKS:
            for i, (own_half, _) in enumerate(chunks):
                if own_half == half:
                    enter_copy(mask, i).wait_recv()
            held = read(got_enter[mask - 1, half], peer(mask) + RANKS * half, held)
    square, linear = held
    sums[0:1, :] = jnp.sum(jnp.transpose(square), axis=0, keepdims=True)
    sums[1:2, :] = jnp.sum(jnp.transpose(linear), axis=0, keepdims=True)
    head_copy = copy(sums, sums_other, sh, rh, {"head": other_head})
    head_copy.start()

    def tell_wait(offset, _):
        tell(offset).wait()
        return 0

    lax.fori_loop(1, count, tell_wait, 0)

    def fold(offset, carry):
        link = box[offset]
        return jnp.where(offset > me, link[1:2] + link[0:1] * carry, carry)

    carry = lax.fori_loop(1, count, fold, jnp.zeros((1, 128), F32))
    reward_total = local_sum + open_row * jnp.concatenate([carry, carry], axis=1)

    for i in range(len(chunks)):
        for mask in MASKS:
            gather_copy(mask, i).wait_send()
            enter_copy(mask, i).wait_send()

    @pl.when(square_first < last_square)
    def _():
        for i in range(len(chunks)):
            pass_copy(i).wait_send()

    head_copy.wait()
    both = sums[...] + sums_other[...]
    value = both[1:2] / jnp.sqrt(both[0:1] / (HEADS * HEAD_DIM) + NORM_EPSILON)
    out[0:1, :] = value
    out[1:2, :] = reward_total - value


def local(count, features, b_input, c_input, step_input, decay_log, skip_gain, norm_gain, value_weight, rewards, keep, ends):
    dma = pltpu.SemaphoreType.DMA
    pieces = PARTS * SPLIT
    quarter = (PARTS, 128, 128)
    operands = (
        features, b_input, c_input, step_input,
        decay_log.reshape(1, -1), skip_gain.reshape(1, -1), norm_gain.reshape(1, -1), value_weight.reshape(1, -1),
        rewards.reshape(1, -1), keep.reshape(1, -1), ends.reshape(1, -1),
    )
    result = pl.pallas_call(
        functools.partial(kernel, count),
        out_shape=jax.ShapeDtypeStruct((2, SPAN), F32),
        in_specs=[pl.BlockSpec(memory_space=pl.ANY)] * 11,
        out_specs=pl.BlockSpec(memory_space=pltpu.VMEM),
        scratch_shapes=[
            *[pltpu.VMEM(one.shape, one.dtype) for one in operands],
            dma((11,)),
            pltpu.VMEM((64, SPAN), F32),
            pltpu.VMEM((SPAN, 1024), F32),
            pltpu.VMEM((SPAN, 1024), F32),
            pltpu.VMEM((SPAN, SPAN), F32),
            pltpu.VMEM((GROUPS, HEAD_ROWS + 128, 128), F32),
            pltpu.VMEM((RANKS, PARTS, HEAD_ROWS + 128, 128), F32),
            pltpu.VMEM(quarter, F32),
            pltpu.VMEM(quarter, F32),
            pltpu.VMEM((RANKS, *quarter), F32),
            pltpu.VMEM((RANKS - 1, *quarter), F32),
            pltpu.VMEM((GROUPS, 128), F32),
            pltpu.VMEM((count, 8, 128), F32),
            pltpu.VMEM((8, 128), F32),
            pltpu.VMEM((8, SPAN), F32),
            pltpu.VMEM((8, SPAN), F32),
            dma((RANKS - 1, pieces)), dma((RANKS - 1, pieces)),
            dma((pieces,)), dma((pieces,)),
            dma((RANKS - 1, pieces)), dma((RANKS - 1, pieces)),
            dma((count,)), dma((count,)),
            dma, dma,
        ],
        compiler_params=pltpu.CompilerParams(
            collective_id=0, has_side_effects=True, vmem_limit_bytes=67043328
        ),
    )(*operands)
    return (result[0], result[1])


def solution(mesh):
    tokens = P(("traj", "ctx"))
    placed = (
        P(("traj", "ctx"), "head"),
        P(("traj", "ctx"), None),
        P(("traj", "ctx"), None),
        P("head", ("traj", "ctx")),
        P("head"), P("head"), P("head"), P("head"),
        tokens, tokens, tokens,
    )
    return jax.shard_map(
        functools.partial(local, mesh.shape["ctx"]),
        mesh=mesh,
        in_specs=placed,
        out_specs=(tokens, tokens),
        check_vma=False,
    )
```

```python
import functools

import jax
import jax.numpy as jnp
from jax import lax
from jax.experimental import pallas as pl
from jax.experimental.pallas import tpu as pltpu
from jax.sharding import PartitionSpec as P

HEADS = 64
HEAD_DIM = 32
SPAN = 256
NORM_EPSILON = 1e-05
FULL = lax.Precision.HIGHEST
MESH = pl.DeviceIdType.MESH
F32 = jnp.float32
BF16 = jnp.bfloat16
GROUPS = 8
RANKS = 4
PARTS = GROUPS // RANKS
SPLIT = 2
ROWS = 128 // SPLIT
HEAD_ROWS = 8
MASKS = (3, 1, 2)
EARLY = 5


def thirds(x):
    hi = x.astype(BF16)
    rest = x - hi.astype(F32)
    mid = rest.astype(BF16)
    lo = (rest - mid.astype(F32)).astype(BF16)
    return hi, mid, lo


def dot(a, b):
    return jnp.dot(a, b, preferred_element_type=F32)


def row_to_column(row, size):
    eye = lax.broadcasted_iota(jnp.int32, (size, size), 0) == lax.broadcasted_iota(jnp.int32, (size, size), 1)
    return jnp.sum(jnp.where(eye, jnp.broadcast_to(row, (size, size)), 0.0), axis=1, keepdims=True)


def kernel(
    count,
    *refs,
):
    sources, (out, *scratch) = refs[:11], refs[11:]
    here, sem_in = scratch[:11], scratch[11]
    run(count, sources, sem_in, out, *here, *scratch[12:])


def run(
    count, sources, sem_in, out,
    feat, b_in, c_in, step_in, decay_log, skip, gain, weight, rewards, keep, ends,
    rows, expl, base, scores, state, square_state, passed, got_passed, enter, got_enter, read_rows,
    box, note, sums, sums_other,
    s1, r1, s2, r2, s3, r3, sn, rn, sh, rh,
):
    held_here = (feat, b_in, c_in, step_in, decay_log, skip, gain, weight, rewards, keep, ends)
    loads = [pltpu.make_async_copy(sources[i], held_here[i], sem_in.at[i]) for i in range(11)]
    for i in (3, 4, 0, 1, 2, 5, 6, 7, 8, 9, 10):
        loads[i].start()
    me = lax.axis_index("ctx")
    rank = lax.rem(me, RANKS)
    square_first = me - rank
    last_square = count - RANKS
    other_head = 1 - lax.axis_index("head")

    def peer(mask):
        return jnp.bitwise_xor(rank, mask)

    barrier = pltpu.get_barrier_semaphore()

    def greet(offset, _):
        pl.semaphore_signal(barrier, inc=1, device_id={"ctx": lax.rem(me + offset, count)}, device_id_type=MESH)
        return 0

    lax.fori_loop(1, count, greet, 0)
    pl.semaphore_signal(barrier, inc=1, device_id={"head": other_head}, device_id_type=MESH)

    row_i = lax.broadcasted_iota(jnp.int32, (SPAN, SPAN), 0)
    col_i = lax.broadcasted_iota(jnp.int32, (SPAN, SPAN), 1)
    upto = (row_i <= col_i).astype(BF16)
    pick_row = lax.broadcasted_iota(jnp.int32, (128, 512), 0)
    pick_head = lax.broadcasted_iota(jnp.int32, (128, 512), 1) // HEAD_DIM
    pick_low = jnp.where(pick_row < 96, lax.rem(pick_row, 32), -1)

    def pick(half):
        return (pick_low == pick_head + 16 * half).astype(BF16)

    loads[3].wait()
    loads[4].wait()
    step = jax.nn.softplus(step_in[...])
    log_decay = -jnp.exp(row_to_column(decay_log[...], 32)) * step
    cum_parts = dot(jnp.concatenate(thirds(log_decay), axis=0), upto)
    cum = cum_parts[0:32] + cum_parts[32:64] + cum_parts[64:96]
    total = cum[:, SPAN - 1 : SPAN]
    rows[0:32, :] = cum
    rows[32:64, :] = step
    none = jnp.zeros((32, SPAN), BF16)

    def columns_of(values):
        stacked = jnp.concatenate([*thirds(values), none], axis=0)
        return jnp.transpose(stacked.astype(F32)).astype(BF16)

    scale_cols = columns_of(jnp.exp(total - cum) * step)
    grow_cols = columns_of(jnp.exp(cum))

    loads[0].wait()
    loads[1].wait()
    keys = jnp.transpose(b_in[...].astype(F32)).astype(BF16)

    def copy(src, dst, send, recv, where):
        return pltpu.make_async_remote_copy(
            src_ref=src, dst_ref=dst, send_sem=send, recv_sem=recv, device_id=where, device_id_type=MESH
        )

    def state_rows(part):
        first = HEAD_ROWS + part * ROWS
        return pl.ds(0, HEAD_ROWS + ROWS) if part == 0 else pl.ds(first, ROWS)

    def plain_rows(part):
        return pl.ds(part * ROWS, ROWS)

    chunks = [(half, part) for half in range(PARTS) for part in range(SPLIT)]

    def gather_copy(mask, i):
        half, part = chunks[i]
        at = state_rows(part)
        return copy(
            state.at[peer(mask) + RANKS * half, at], square_state.at[rank, half, at],
            s1.at[mask - 1, i], r1.at[mask - 1, i], {"ctx": square_first + peer(mask)},
        )

    def pass_copy(i):
        half, part = chunks[i]
        at = plain_rows(part)
        return copy(
            passed.at[half, at], got_passed.at[half, at], s2.at[i], r2.at[i], {"ctx": lax.rem(me + RANKS, count)}
        )

    def enter_copy(mask, i):
        half, part = chunks[i]
        at = plain_rows(part)
        return copy(
            enter.at[peer(mask), half, at], got_enter.at[mask - 1, half, at],
            s3.at[mask - 1, i], r3.at[mask - 1, i], {"ctx": square_first + peer(mask)},
        )

    for half in range(PARTS):
        at = slice(512 * half, 512 * half + 512)
        chosen = pick(half)
        scaled = (dot(scale_cols, chosen) * feat[:, at].astype(F32)).astype(BF16)
        block_state = dot(keys, scaled)
        decay = dot(grow_cols[SPAN - 16 : SPAN], chosen)[8:16]
        for g in range(RANKS):
            lanes = slice(128 * g, 128 * g + 128)
            state[RANKS * half + g, 0:HEAD_ROWS] = decay[:, lanes]
            state[RANKS * half + g, HEAD_ROWS : HEAD_ROWS + 128] = block_state[:, lanes]
        if half == 0:
            pl.semaphore_wait(barrier, count)
        for i, (own_half, _) in enumerate(chunks):
            if own_half == half:
                for mask in MASKS:
                    gather_copy(mask, i).start()
        square_state[rank, half] = state[rank + RANKS * half]

    for half in range(PARTS):
        expl[:, 512 * half : 512 * half + 512] = dot(grow_cols, pick(half))
    for i in (2, 5, 6, 7, 8, 9, 10):
        loads[i].wait()

    live = keep[...].astype(F32) * rewards[...]
    end_row = ends[...].astype(F32)
    end_rows = jnp.broadcast_to(end_row, (8, SPAN)).astype(BF16)
    before = dot(end_rows, (row_i < col_i).astype(BF16))[0:1]
    end_total = before[:, SPAN - 1 : SPAN] + end_row[:, SPAN - 1 : SPAN]
    reach = ((row_i >= col_i) & (row_to_column(before, SPAN) == before)).astype(F32)
    local_sum = jnp.dot(
        jnp.broadcast_to(live, (8, SPAN)), reach, precision=FULL, preferred_element_type=F32
    )[0:1]
    open_row = (before == end_total).astype(F32)
    note[0:1, :] = jnp.broadcast_to(open_row[:, 0:1], (1, 128))
    note[1:2, :] = jnp.broadcast_to(local_sum[:, 0:1], (1, 128))
    note[2:8, :] = jnp.zeros((6, 128), F32)

    def tell(offset):
        return copy(note, box.at[offset], sn.at[offset], rn.at[offset], {"ctx": lax.rem(me + offset, count)})

    def tell_start(offset, _):
        tell(offset).start()
        return 0

    lax.fori_loop(1, count, tell_start, 0)

    scores[...] = lax.dot_general(c_in[...], b_in[...], (((1,), (1,)), ((), ())), preferred_element_type=F32)
    skip_cols = jnp.broadcast_to(skip[...], (8, 32))
    skip_parts = jnp.concatenate([*(one.astype(F32) for one in thirds(skip_cols)), jnp.zeros((8, 32), F32)], axis=1)
    for half in range(2):
        skip_lanes = dot(skip_parts.astype(BF16), pick(half))
        at = slice(512 * half, 512 * half + 512)
        base[:, at] = skip_lanes[0:1] * feat[:, at].astype(F32)
    causal = row_i[0:128, 0:128] >= col_i[0:128, 0:128]
    lane_head = lax.broadcasted_iota(jnp.int32, (SPAN, 128), 1) // HEAD_DIM

    def intra(unit):
        at = slice(unit * 128, unit * 128 + 128)
        aligned = unit // 2 * 8
        cum_rows = rows[aligned : 8 + aligned, :]
        step_rows = rows[32 + aligned : 40 + aligned, :]
        cum_cols = jnp.transpose(cum_rows)
        values = feat[:, at].astype(F32)
        top = base[0:128, at]
        low = base[128:256, at]
        for lane_h in range(4):
            h = lane_h + unit % 2 * 4
            masked = jnp.where(lane_head == lane_h, values, 0.0).astype(BF16)
            c_t0, c_t1 = cum_cols[0:128, h : h + 1], cum_cols[128:256, h : h + 1]
            c_s0, c_s1 = cum_rows[h : h + 1, 0:128], cum_rows[h : h + 1, 128:256]
            d_s0, d_s1 = step_rows[h : h + 1, 0:128], step_rows[h : h + 1, 128:256]
            w_tl = jnp.where(causal, scores[0:128, 0:128] * jnp.exp(c_t0 - c_s0) * d_s0, 0.0).astype(BF16)
            w_bl = (scores[128:256, 0:128] * jnp.exp(c_t1 - c_s0) * d_s0).astype(BF16)
            w_br = jnp.where(causal, scores[128:256, 128:256] * jnp.exp(c_t1 - c_s1) * d_s1, 0.0).astype(BF16)
            top = top + dot(w_tl, masked[0:128])
            low = low + dot(jnp.concatenate([w_bl, w_br], axis=1), masked)
        base[0:128, at] = top
        base[128:256, at] = low

    def rest():
        for unit in range(EARLY, GROUPS):
            intra(unit)

    for unit in range(EARLY):
        intra(unit)
    pl.when(square_first > 0)(rest)

    for i, (half, part) in enumerate(chunks):
        for mask in MASKS:
            gather_copy(mask, i).wait_recv()
        held = pl.ds(HEAD_ROWS + part * ROWS, ROWS)
        at = plain_rows(part)
        blocks = [square_state[k, half, held] for k in range(RANKS)]
        decays = [square_state[k, half, HEAD_ROWS - 1 : HEAD_ROWS] for k in range(RANKS)]

        @pl.when(square_first == 0)
        def _():
            second = blocks[0]
            third = decays[1] * second + blocks[1]
            fourth = decays[2] * third + blocks[2]
            passed[half, at] = decays[3] * fourth + blocks[3]
            pass_copy(i).start()
            enter[0, half, at] = jnp.zeros_like(second)
            enter[1, half, at] = second
            enter[2, half, at] = third
            enter[3, half, at] = fourth

        @pl.when(square_first > 0)
        def _():
            pass_copy(i).wait_recv()
            first = got_passed[half, at]
            second = decays[0] * first + blocks[0]
            third = decays[1] * second + blocks[1]
            fourth = decays[2] * third + blocks[2]

            @pl.when(square_first < last_square)
            def _():
                passed[half, at] = decays[3] * fourth + blocks[3]
                pass_copy(i).start()

            enter[0, half, at] = first
            enter[1, half, at] = second
            enter[2, half, at] = third
            enter[3, half, at] = fourth

        @pl.when(square_first > 0)
        def _():
            for mask in MASKS:
                enter_copy(mask, i).start()

    @pl.when(square_first == 0)
    def _():
        for i in range(len(chunks)):
            for mask in MASKS:
                enter_copy(mask, i).start()
        rest()

    queries = c_in[...]
    readout = weight[...] * gain[...]
    sums[...] = jnp.zeros((8, SPAN), F32)
    for g in range(GROUPS):
        read_rows[g : g + 1, :] = readout[:, 128 * g : 128 * g + 128]

    def read(entering, group, held):
        square, linear = held
        hi, mid, _ = thirds(entering)
        carried = dot(queries, hi) + dot(queries, mid)
        at = pl.ds(pl.multiple_of(group * 128, 128), 128)
        mixed = base[:, at] + expl[:, at] * carried
        return square + mixed * mixed, linear + mixed * read_rows[pl.ds(group, 1), :]

    zero = jnp.zeros((SPAN, 128), F32)
    held = (zero, zero)
    for half in range(PARTS):
        held = read(enter[rank, half], rank + RANKS * half, held)
    for half in range(PARTS):
        for mask in MASKS:
            for i, (own_half, _) in enumerate(chunks):
                if own_half == half:
                    enter_copy(mask, i).wait_recv()
            held = read(got_enter[mask - 1, half], peer(mask) + RANKS * half, held)
    square, linear = held
    sums[0:1, :] = jnp.sum(jnp.transpose(square), axis=0, keepdims=True)
    sums[1:2, :] = jnp.sum(jnp.transpose(linear), axis=0, keepdims=True)
    head_copy = copy(sums, sums_other, sh, rh, {"head": other_head})
    head_copy.start()

    def tell_wait(offset, _):
        tell(offset).wait()
        return 0

    lax.fori_loop(1, count, tell_wait, 0)

    def fold(offset, carry):
        link = box[offset]
        return jnp.where(offset > me, link[1:2] + link[0:1] * carry, carry)

    carry = lax.fori_loop(1, count, fold, jnp.zeros((1, 128), F32))
    reward_total = local_sum + open_row * jnp.concatenate([carry, carry], axis=1)

    for i in range(len(chunks)):
        for mask in MASKS:
            gather_copy(mask, i).wait_send()
            enter_copy(mask, i).wait_send()

    @pl.when(square_first < last_square)
    def _():
        for i in range(len(chunks)):
            pass_copy(i).wait_send()

    head_copy.wait()
    both = sums[...] + sums_other[...]
    value = both[1:2] / jnp.sqrt(both[0:1] / (HEADS * HEAD_DIM) + NORM_EPSILON)
    out[0:1, :] = value
    out[1:2, :] = reward_total - value


def local(count, features, b_input, c_input, step_input, decay_log, skip_gain, norm_gain, value_weight, rewards, keep, ends):
    dma = pltpu.SemaphoreType.DMA
    pieces = PARTS * SPLIT
    quarter = (PARTS, 128, 128)
    operands = (
        features, b_input, c_input, step_input,
        decay_log.reshape(1, -1), skip_gain.reshape(1, -1), norm_gain.reshape(1, -1), value_weight.reshape(1, -1),
        rewards.reshape(1, -1), keep.reshape(1, -1), ends.reshape(1, -1),
    )
    result = pl.pallas_call(
        functools.partial(kernel, count),
        out_shape=jax.ShapeDtypeStruct((2, SPAN), F32),
        in_specs=[pl.BlockSpec(memory_space=pl.ANY)] * 11,
        out_specs=pl.BlockSpec(memory_space=pltpu.VMEM),
        scratch_shapes=[
            *[pltpu.VMEM(one.shape, one.dtype) for one in operands],
            dma((11,)),
            pltpu.VMEM((64, SPAN), F32),
            pltpu.VMEM((SPAN, 1024), F32),
            pltpu.VMEM((SPAN, 1024), F32),
            pltpu.VMEM((SPAN, SPAN), F32),
            pltpu.VMEM((GROUPS, HEAD_ROWS + 128, 128), F32),
            pltpu.VMEM((RANKS, PARTS, HEAD_ROWS + 128, 128), F32),
            pltpu.VMEM(quarter, F32),
            pltpu.VMEM(quarter, F32),
            pltpu.VMEM((RANKS, *quarter), F32),
            pltpu.VMEM((RANKS - 1, *quarter), F32),
            pltpu.VMEM((GROUPS, 128), F32),
            pltpu.VMEM((count, 8, 128), F32),
            pltpu.VMEM((8, 128), F32),
            pltpu.VMEM((8, SPAN), F32),
            pltpu.VMEM((8, SPAN), F32),
            dma((RANKS - 1, pieces)), dma((RANKS - 1, pieces)),
            dma((pieces,)), dma((pieces,)),
            dma((RANKS - 1, pieces)), dma((RANKS - 1, pieces)),
            dma((count,)), dma((count,)),
            dma, dma,
        ],
        compiler_params=pltpu.CompilerParams(
            collective_id=0, has_side_effects=True, vmem_limit_bytes=67043328
        ),
    )(*operands)
    return (result[0], result[1])


def solution(mesh):
    tokens = P(("traj", "ctx"))
    placed = (
        P(("traj", "ctx"), "head"),
        P(("traj", "ctx"), None),
        P(("traj", "ctx"), None),
        P("head", ("traj", "ctx")),
        P("head"), P("head"), P("head"), P("head"),
        tokens, tokens, tokens,
    )
    return jax.shard_map(
        functools.partial(local, mesh.shape["ctx"]),
        mesh=mesh,
        in_specs=placed,
        out_specs=(tokens, tokens),
        check_vma=False,
    )
```

```python
import functools

import jax
import jax.numpy as jnp
from jax import lax
from jax.experimental import pallas as pl
from jax.experimental.pallas import tpu as pltpu
from jax.sharding import PartitionSpec as P

HEADS = 64
HEAD_DIM = 32
SPAN = 256
NORM_EPSILON = 1e-05
FULL = lax.Precision.HIGHEST
MESH = pl.DeviceIdType.MESH
F32 = jnp.float32
BF16 = jnp.bfloat16
GROUPS = 8
RANKS = 4
PARTS = GROUPS // RANKS
SPLIT = 2
ROWS = 128 // SPLIT
HEAD_ROWS = 8
MASKS = (3, 1, 2)
EARLY = 5


def thirds(x):
    hi = x.astype(BF16)
    rest = x - hi.astype(F32)
    mid = rest.astype(BF16)
    lo = (rest - mid.astype(F32)).astype(BF16)
    return hi, mid, lo


def dot(a, b):
    return jnp.dot(a, b, preferred_element_type=F32)


def row_to_column(row, size):
    eye = lax.broadcasted_iota(jnp.int32, (size, size), 0) == lax.broadcasted_iota(jnp.int32, (size, size), 1)
    return jnp.sum(jnp.where(eye, jnp.broadcast_to(row, (size, size)), 0.0), axis=1, keepdims=True)


def kernel(
    count,
    *refs,
):
    sources, (out, *scratch) = refs[:11], refs[11:]
    here, sem_in = scratch[:11], scratch[11]
    run(count, sources, sem_in, out, *here, *scratch[12:])


def run(
    count, sources, sem_in, out,
    feat, b_in, c_in, step_in, decay_log, skip, gain, weight, rewards, keep, ends,
    rows, expl, base, scores, state, square_state, passed, got_passed, enter, got_enter, read_rows,
    box, note, later, got_later, sums, sums_other,
    s1, r1, s2, r2, s3, r3, sn, rn, sh, rh, ready,
):
    held_here = (feat, b_in, c_in, step_in, decay_log, skip, gain, weight, rewards, keep, ends)
    loads = [pltpu.make_async_copy(sources[i], held_here[i], sem_in.at[i]) for i in range(11)]
    for i in (3, 4, 0, 1, 2, 5, 6, 7, 8, 9, 10):
        loads[i].start()
    me = lax.axis_index("ctx")
    rank = lax.rem(me, RANKS)
    square_first = me - rank
    last_square = count - RANKS
    other_head = 1 - lax.axis_index("head")

    def peer(mask):
        return jnp.bitwise_xor(rank, mask)

    barrier = pltpu.get_barrier_semaphore()

    for mask in MASKS:
        pl.semaphore_signal(barrier, inc=1, device_id={"ctx": square_first + peer(mask)}, device_id_type=MESH)
    pl.semaphore_signal(barrier, inc=1, device_id={"head": other_head}, device_id_type=MESH)

    @pl.when(square_first < last_square)
    def _():
        pl.semaphore_signal(barrier, inc=1, device_id={"ctx": me + RANKS}, device_id_type=MESH)

    row_i = lax.broadcasted_iota(jnp.int32, (SPAN, SPAN), 0)
    col_i = lax.broadcasted_iota(jnp.int32, (SPAN, SPAN), 1)
    upto = (row_i <= col_i).astype(BF16)
    pick_row = lax.broadcasted_iota(jnp.int32, (128, 512), 0)
    pick_head = lax.broadcasted_iota(jnp.int32, (128, 512), 1) // HEAD_DIM
    pick_low = jnp.where(pick_row < 96, lax.rem(pick_row, 32), -1)

    def pick(half):
        return (pick_low == pick_head + 16 * half).astype(BF16)

    loads[3].wait()
    loads[4].wait()
    step = jax.nn.softplus(step_in[...])
    log_decay = -jnp.exp(row_to_column(decay_log[...], 32)) * step
    cum_parts = dot(jnp.concatenate(thirds(log_decay), axis=0), upto)
    cum = cum_parts[0:32] + cum_parts[32:64] + cum_parts[64:96]
    total = cum[:, SPAN - 1 : SPAN]
    rows[0:32, :] = cum
    rows[32:64, :] = step
    none = jnp.zeros((32, SPAN), BF16)

    def columns_of(values):
        stacked = jnp.concatenate([*thirds(values), none], axis=0)
        return jnp.transpose(stacked.astype(F32)).astype(BF16)

    scale_cols = columns_of(jnp.exp(total - cum) * step)
    grow_cols = columns_of(jnp.exp(cum))

    loads[0].wait()
    loads[1].wait()
    keys = jnp.transpose(b_in[...].astype(F32)).astype(BF16)

    def copy(src, dst, send, recv, where):
        return pltpu.make_async_remote_copy(
            src_ref=src, dst_ref=dst, send_sem=send, recv_sem=recv, device_id=where, device_id_type=MESH
        )

    def state_rows(part):
        first = HEAD_ROWS + part * ROWS
        return pl.ds(0, HEAD_ROWS + ROWS) if part == 0 else pl.ds(first, ROWS)

    def plain_rows(part):
        return pl.ds(part * ROWS, ROWS)

    chunks = [(half, part) for half in range(PARTS) for part in range(SPLIT)]

    def gather_copy(mask, i):
        half, part = chunks[i]
        at = state_rows(part)
        return copy(
            state.at[peer(mask) + RANKS * half, at], square_state.at[rank, half, at],
            s1.at[mask - 1, i], r1.at[mask - 1, i], {"ctx": square_first + peer(mask)},
        )

    def pass_copy(i):
        half, part = chunks[i]
        at = plain_rows(part)
        return copy(
            passed.at[half, at], got_passed.at[half, at], s2.at[i], r2.at[i], {"ctx": lax.rem(me + RANKS, count)}
        )

    def enter_copy(mask, i):
        half, part = chunks[i]
        at = plain_rows(part)
        return copy(
            enter.at[peer(mask), half, at], got_enter.at[mask - 1, half, at],
            s3.at[mask - 1, i], r3.at[mask - 1, i], {"ctx": square_first + peer(mask)},
        )

    for half in range(PARTS):
        at = slice(512 * half, 512 * half + 512)
        chosen = pick(half)
        scaled = (dot(scale_cols, chosen) * feat[:, at].astype(F32)).astype(BF16)
        block_state = dot(keys, scaled)
        decay = dot(grow_cols[SPAN - 16 : SPAN], chosen)[8:16]
        for g in range(RANKS):
            lanes = slice(128 * g, 128 * g + 128)
            state[RANKS * half + g, 0:HEAD_ROWS] = decay[:, lanes]
            state[RANKS * half + g, HEAD_ROWS : HEAD_ROWS + 128] = block_state[:, lanes]
        if half == 0:
            pl.semaphore_wait(barrier, RANKS + jnp.where(square_first > 0, 1, 0))

            @pl.when(square_first > 0)
            def _():
                pl.semaphore_signal(ready, inc=1, device_id={"ctx": me - RANKS}, device_id_type=MESH)
        for i, (own_half, _) in enumerate(chunks):
            if own_half == half:
                for mask in MASKS:
                    gather_copy(mask, i).start()
        square_state[rank, half] = state[rank + RANKS * half]

    for half in range(PARTS):
        expl[:, 512 * half : 512 * half + 512] = dot(grow_cols, pick(half))
    for i in (2, 5, 6, 7, 8, 9, 10):
        loads[i].wait()

    live = keep[...].astype(F32) * rewards[...]
    end_row = ends[...].astype(F32)
    end_rows = jnp.broadcast_to(end_row, (8, SPAN)).astype(BF16)
    before = dot(end_rows, (row_i < col_i).astype(BF16))[0:1]
    end_total = before[:, SPAN - 1 : SPAN] + end_row[:, SPAN - 1 : SPAN]
    reach = ((row_i >= col_i) & (row_to_column(before, SPAN) == before)).astype(F32)
    local_sum = jnp.dot(
        jnp.broadcast_to(live, (8, SPAN)), reach, precision=FULL, preferred_element_type=F32
    )[0:1]
    open_row = (before == end_total).astype(F32)
    note[0:1, :] = jnp.broadcast_to(open_row[:, 0:1], (1, 128))
    note[1:2, :] = jnp.broadcast_to(local_sum[:, 0:1], (1, 128))
    note[2:8, :] = jnp.zeros((6, 128), F32)

    def tell(mask):
        return copy(note, box.at[mask], sn.at[mask], rn.at[mask], {"ctx": square_first + peer(mask)})

    def tell_back():
        return copy(later, got_later, sn.at[0], rn.at[0], {"ctx": me - RANKS})

    for mask in MASKS:
        tell(mask).start()

    scores[...] = lax.dot_general(c_in[...], b_in[...], (((1,), (1,)), ((), ())), preferred_element_type=F32)
    skip_cols = jnp.broadcast_to(skip[...], (8, 32))
    skip_parts = jnp.concatenate([*(one.astype(F32) for one in thirds(skip_cols)), jnp.zeros((8, 32), F32)], axis=1)
    for half in range(2):
        skip_lanes = dot(skip_parts.astype(BF16), pick(half))
        at = slice(512 * half, 512 * half + 512)
        base[:, at] = skip_lanes[0:1] * feat[:, at].astype(F32)
    causal = row_i[0:128, 0:128] >= col_i[0:128, 0:128]
    lane_head = lax.broadcasted_iota(jnp.int32, (SPAN, 128), 1) // HEAD_DIM

    def intra(unit):
        at = slice(unit * 128, unit * 128 + 128)
        aligned = unit // 2 * 8
        cum_rows = rows[aligned : 8 + aligned, :]
        step_rows = rows[32 + aligned : 40 + aligned, :]
        cum_cols = jnp.transpose(cum_rows)
        values = feat[:, at].astype(F32)
        top = base[0:128, at]
        low = base[128:256, at]
        for lane_h in range(4):
            h = lane_h + unit % 2 * 4
            masked = jnp.where(lane_head == lane_h, values, 0.0).astype(BF16)
            c_t0, c_t1 = cum_cols[0:128, h : h + 1], cum_cols[128:256, h : h + 1]
            c_s0, c_s1 = cum_rows[h : h + 1, 0:128], cum_rows[h : h + 1, 128:256]
            d_s0, d_s1 = step_rows[h : h + 1, 0:128], step_rows[h : h + 1, 128:256]
            w_tl = jnp.where(causal, scores[0:128, 0:128] * jnp.exp(c_t0 - c_s0) * d_s0, 0.0).astype(BF16)
            w_bl = (scores[128:256, 0:128] * jnp.exp(c_t1 - c_s0) * d_s0).astype(BF16)
            w_br = jnp.where(causal, scores[128:256, 128:256] * jnp.exp(c_t1 - c_s1) * d_s1, 0.0).astype(BF16)
            top = top + dot(w_tl, masked[0:128])
            low = low + dot(jnp.concatenate([w_bl, w_br], axis=1), masked)
        base[0:128, at] = top
        base[128:256, at] = low

    def rest():
        for unit in range(EARLY, GROUPS):
            intra(unit)

    for unit in range(EARLY):
        intra(unit)
    pl.when(square_first > 0)(rest)

    @pl.when(square_first < last_square)
    def _():
        pl.semaphore_wait(ready, 1)

    for i, (half, part) in enumerate(chunks):
        for mask in MASKS:
            gather_copy(mask, i).wait_recv()
        held = pl.ds(HEAD_ROWS + part * ROWS, ROWS)
        at = plain_rows(part)
        blocks = [square_state[k, half, held] for k in range(RANKS)]
        decays = [square_state[k, half, HEAD_ROWS - 1 : HEAD_ROWS] for k in range(RANKS)]

        @pl.when(square_first == 0)
        def _():
            second = blocks[0]
            third = decays[1] * second + blocks[1]
            fourth = decays[2] * third + blocks[2]
            passed[half, at] = decays[3] * fourth + blocks[3]
            pass_copy(i).start()
            enter[0, half, at] = jnp.zeros_like(second)
            enter[1, half, at] = second
            enter[2, half, at] = third
            enter[3, half, at] = fourth

        @pl.when(square_first > 0)
        def _():
            pass_copy(i).wait_recv()
            first = got_passed[half, at]
            second = decays[0] * first + blocks[0]
            third = decays[1] * second + blocks[1]
            fourth = decays[2] * third + blocks[2]

            @pl.when(square_first < last_square)
            def _():
                passed[half, at] = decays[3] * fourth + blocks[3]
                pass_copy(i).start()

            enter[0, half, at] = first
            enter[1, half, at] = second
            enter[2, half, at] = third
            enter[3, half, at] = fourth

        @pl.when(square_first > 0)
        def _():
            for mask in MASKS:
                enter_copy(mask, i).start()

    @pl.when(square_first == 0)
    def _():
        for i in range(len(chunks)):
            for mask in MASKS:
                enter_copy(mask, i).start()
        rest()

    for mask in MASKS:
        tell(mask).wait()
    box[0] = note[...]

    @pl.when(square_first == last_square)
    def _():
        got_later[...] = jnp.zeros((8, 128), F32)

    @pl.when(square_first < last_square)
    def _():
        tell_back().wait_recv()

    carry = got_later[1:2, :]
    whole = carry
    for k in range(RANKS - 1, -1, -1):
        link = box[jnp.bitwise_xor(rank, k)]
        whole = link[1:2] + link[0:1] * whole
        carry = jnp.where(k > rank, whole, carry)
    later[...] = jnp.broadcast_to(whole, (8, 128))

    @pl.when(square_first > 0)
    def _():
        tell_back().start()


    queries = c_in[...]
    readout = weight[...] * gain[...]
    sums[...] = jnp.zeros((8, SPAN), F32)
    for g in range(GROUPS):
        read_rows[g : g + 1, :] = readout[:, 128 * g : 128 * g + 128]

    def read(entering, group, held):
        square, linear = held
        hi, mid, _ = thirds(entering)
        carried = dot(queries, hi) + dot(queries, mid)
        at = pl.ds(pl.multiple_of(group * 128, 128), 128)
        mixed = base[:, at] + expl[:, at] * carried
        return square + mixed * mixed, linear + mixed * read_rows[pl.ds(group, 1), :]

    zero = jnp.zeros((SPAN, 128), F32)
    held = (zero, zero)
    for half in range(PARTS):
        held = read(enter[rank, half], rank + RANKS * half, held)
    for half in range(PARTS):
        for mask in MASKS:
            for i, (own_half, _) in enumerate(chunks):
                if own_half == half:
                    enter_copy(mask, i).wait_recv()
            held = read(got_enter[mask - 1, half], peer(mask) + RANKS * half, held)
    square, linear = held
    sums[0:1, :] = jnp.sum(jnp.transpose(square), axis=0, keepdims=True)
    sums[1:2, :] = jnp.sum(jnp.transpose(linear), axis=0, keepdims=True)
    head_copy = copy(sums, sums_other, sh, rh, {"head": other_head})
    head_copy.start()

    @pl.when(square_first > 0)
    def _():
        tell_back().wait_send()

    reward_total = local_sum + open_row * jnp.concatenate([carry, carry], axis=1)

    for i in range(len(chunks)):
        for mask in MASKS:
            gather_copy(mask, i).wait_send()
            enter_copy(mask, i).wait_send()

    @pl.when(square_first < last_square)
    def _():
        for i in range(len(chunks)):
            pass_copy(i).wait_send()

    head_copy.wait()
    both = sums[...] + sums_other[...]
    value = both[1:2] / jnp.sqrt(both[0:1] / (HEADS * HEAD_DIM) + NORM_EPSILON)
    out[0:1, :] = value
    out[1:2, :] = reward_total - value


def local(count, features, b_input, c_input, step_input, decay_log, skip_gain, norm_gain, value_weight, rewards, keep, ends):
    dma = pltpu.SemaphoreType.DMA
    pieces = PARTS * SPLIT
    quarter = (PARTS, 128, 128)
    operands = (
        features, b_input, c_input, step_input,
        decay_log.reshape(1, -1), skip_gain.reshape(1, -1), norm_gain.reshape(1, -1), value_weight.reshape(1, -1),
        rewards.reshape(1, -1), keep.reshape(1, -1), ends.reshape(1, -1),
    )
    result = pl.pallas_call(
        functools.partial(kernel, count),
        out_shape=jax.ShapeDtypeStruct((2, SPAN), F32),
        in_specs=[pl.BlockSpec(memory_space=pl.ANY)] * 11,
        out_specs=pl.BlockSpec(memory_space=pltpu.VMEM),
        scratch_shapes=[
            *[pltpu.VMEM(one.shape, one.dtype) for one in operands],
            dma((11,)),
            pltpu.VMEM((64, SPAN), F32),
            pltpu.VMEM((SPAN, 1024), F32),
            pltpu.VMEM((SPAN, 1024), F32),
            pltpu.VMEM((SPAN, SPAN), F32),
            pltpu.VMEM((GROUPS, HEAD_ROWS + 128, 128), F32),
            pltpu.VMEM((RANKS, PARTS, HEAD_ROWS + 128, 128), F32),
            pltpu.VMEM(quarter, F32),
            pltpu.VMEM(quarter, F32),
            pltpu.VMEM((RANKS, *quarter), F32),
            pltpu.VMEM((RANKS - 1, *quarter), F32),
            pltpu.VMEM((GROUPS, 128), F32),
            pltpu.VMEM((RANKS, 8, 128), F32),
            pltpu.VMEM((8, 128), F32),
            pltpu.VMEM((8, 128), F32),
            pltpu.VMEM((8, 128), F32),
            pltpu.VMEM((8, SPAN), F32),
            pltpu.VMEM((8, SPAN), F32),
            dma((RANKS - 1, pieces)), dma((RANKS - 1, pieces)),
            dma((pieces,)), dma((pieces,)),
            dma((RANKS - 1, pieces)), dma((RANKS - 1, pieces)),
            dma((RANKS,)), dma((RANKS,)),
            dma, dma,
            pltpu.SemaphoreType.REGULAR,
        ],
        compiler_params=pltpu.CompilerParams(
            collective_id=0, has_side_effects=True, vmem_limit_bytes=67043328
        ),
    )(*operands)
    return (result[0], result[1])


def solution(mesh):
    tokens = P(("traj", "ctx"))
    placed = (
        P(("traj", "ctx"), "head"),
        P(("traj", "ctx"), None),
        P(("traj", "ctx"), None),
        P("head", ("traj", "ctx")),
        P("head"), P("head"), P("head"), P("head"),
        tokens, tokens, tokens,
    )
    return jax.shard_map(
        functools.partial(local, mesh.shape["ctx"]),
        mesh=mesh,
        in_specs=placed,
        out_specs=(tokens, tokens),
        check_vma=False,
    )
```

```python
import functools

import jax
import jax.numpy as jnp
from jax import lax
from jax.experimental import pallas as pl
from jax.experimental.pallas import tpu as pltpu
from jax.sharding import PartitionSpec as P

HEADS = 64
HEAD_DIM = 32
SPAN = 256
NORM_EPSILON = 1e-05
FULL = lax.Precision.HIGHEST
MESH = pl.DeviceIdType.MESH
F32 = jnp.float32
BF16 = jnp.bfloat16
GROUPS = 8
RANKS = 4
PARTS = GROUPS // RANKS
SPLIT = 2
ROWS = 128 // SPLIT
HEAD_ROWS = 8
MASKS = (3, 1, 2)
EARLY = 5


def thirds(x):
    hi = x.astype(BF16)
    rest = x - hi.astype(F32)
    mid = rest.astype(BF16)
    lo = (rest - mid.astype(F32)).astype(BF16)
    return hi, mid, lo


def dot(a, b):
    return jnp.dot(a, b, preferred_element_type=F32)


def row_to_column(row, size):
    eye = lax.broadcasted_iota(jnp.int32, (size, size), 0) == lax.broadcasted_iota(jnp.int32, (size, size), 1)
    return jnp.sum(jnp.where(eye, jnp.broadcast_to(row, (size, size)), 0.0), axis=1, keepdims=True)


def kernel(
    count,
    *refs,
):
    sources, (out, *scratch) = refs[:11], refs[11:]
    here, sem_in = scratch[:11], scratch[11]
    run(count, sources, sem_in, out, *here, *scratch[12:])


def run(
    count, sources, sem_in, out,
    feat, b_in, c_in, step_in, decay_log, skip, gain, weight, rewards, keep, ends,
    rows, expl, base, scores, state, square_state, passed, got_passed, enter, got_enter, read_rows,
    box, note, later, got_later, sums, sums_other,
    s1, r1, s2, r2, s3, r3, sn, rn, sh, rh, ready,
):
    held_here = (feat, b_in, c_in, step_in, decay_log, skip, gain, weight, rewards, keep, ends)
    loads = [pltpu.make_async_copy(sources[i], held_here[i], sem_in.at[i]) for i in range(11)]
    for i in (3, 4, 0, 1, 2, 5, 6, 7, 8, 9, 10):
        loads[i].start()
    me = lax.axis_index("ctx")
    rank = lax.rem(me, RANKS)
    square_first = me - rank
    last_square = count - RANKS
    other_head = 1 - lax.axis_index("head")

    def peer(mask):
        return jnp.bitwise_xor(rank, mask)

    barrier = pltpu.get_barrier_semaphore()

    for mask in MASKS:
        pl.semaphore_signal(barrier, inc=1, device_id={"ctx": square_first + peer(mask)}, device_id_type=MESH)
    pl.semaphore_signal(barrier, inc=1, device_id={"head": other_head}, device_id_type=MESH)

    @pl.when(square_first < last_square)
    def _():
        pl.semaphore_signal(barrier, inc=1, device_id={"ctx": me + RANKS}, device_id_type=MESH)

    row_i = lax.broadcasted_iota(jnp.int32, (SPAN, SPAN), 0)
    col_i = lax.broadcasted_iota(jnp.int32, (SPAN, SPAN), 1)
    upto = (row_i <= col_i).astype(BF16)
    pick_row = lax.broadcasted_iota(jnp.int32, (128, 512), 0)
    pick_head = lax.broadcasted_iota(jnp.int32, (128, 512), 1) // HEAD_DIM
    pick_low = jnp.where(pick_row < 96, lax.rem(pick_row, 32), -1)

    def pick(half):
        return (pick_low == pick_head + 16 * half).astype(BF16)

    loads[3].wait()
    loads[4].wait()
    step = jax.nn.softplus(step_in[...])
    log_decay = -jnp.exp(row_to_column(decay_log[...], 32)) * step
    cum_parts = dot(jnp.concatenate(thirds(log_decay), axis=0), upto)
    cum = cum_parts[0:32] + cum_parts[32:64] + cum_parts[64:96]
    total = cum[:, SPAN - 1 : SPAN]
    rows[0:32, :] = cum
    rows[32:64, :] = step
    none = jnp.zeros((32, SPAN), BF16)

    def columns_of(values):
        stacked = jnp.concatenate([*thirds(values), none], axis=0)
        return jnp.transpose(stacked.astype(F32)).astype(BF16)

    scale_cols = columns_of(jnp.exp(total - cum) * step)
    grow_cols = columns_of(jnp.exp(cum))

    loads[0].wait()
    loads[1].wait()
    keys = jnp.transpose(b_in[...].astype(F32)).astype(BF16)

    def copy(src, dst, send, recv, where):
        return pltpu.make_async_remote_copy(
            src_ref=src, dst_ref=dst, send_sem=send, recv_sem=recv, device_id=where, device_id_type=MESH
        )

    def state_rows(part):
        first = HEAD_ROWS + part * ROWS
        return pl.ds(0, HEAD_ROWS + ROWS) if part == 0 else pl.ds(first, ROWS)

    def plain_rows(part):
        return pl.ds(part * ROWS, ROWS)

    chunks = [(half, part) for half in range(PARTS) for part in range(SPLIT)]

    def gather_copy(mask, i):
        half, part = chunks[i]
        at = state_rows(part)
        return copy(
            state.at[peer(mask) + RANKS * half, at], square_state.at[rank, half, at],
            s1.at[mask - 1, i], r1.at[mask - 1, i], {"ctx": square_first + peer(mask)},
        )

    def pass_copy(i):
        half, part = chunks[i]
        at = plain_rows(part)
        return copy(
            passed.at[half, at], got_passed.at[half, at], s2.at[i], r2.at[i], {"ctx": lax.rem(me + RANKS, count)}
        )

    def enter_copy(mask, i):
        half, part = chunks[i]
        at = plain_rows(part)
        return copy(
            enter.at[peer(mask), half, at], got_enter.at[mask - 1, half, at],
            s3.at[mask - 1, i], r3.at[mask - 1, i], {"ctx": square_first + peer(mask)},
        )

    for half in range(PARTS):
        at = slice(512 * half, 512 * half + 512)
        chosen = pick(half)
        scaled = (dot(scale_cols, chosen) * feat[:, at].astype(F32)).astype(BF16)
        block_state = dot(keys, scaled)
        decay = dot(grow_cols[SPAN - 16 : SPAN], chosen)[8:16]
        for g in range(RANKS):
            lanes = slice(128 * g, 128 * g + 128)
            state[RANKS * half + g, 0:HEAD_ROWS] = decay[:, lanes]
            state[RANKS * half + g, HEAD_ROWS : HEAD_ROWS + 128] = block_state[:, lanes]
        if half == 0:
            pl.semaphore_wait(barrier, RANKS + jnp.where(square_first > 0, 1, 0))

            @pl.when(square_first > 0)
            def _():
                pl.semaphore_signal(ready, inc=1, device_id={"ctx": me - RANKS}, device_id_type=MESH)
        for i, (own_half, _) in enumerate(chunks):
            if own_half == half:
                for mask in MASKS:
                    gather_copy(mask, i).start()
        square_state[rank, half] = state[rank + RANKS * half]

    for half in range(PARTS):
        expl[:, 512 * half : 512 * half + 512] = dot(grow_cols, pick(half))
    for i in (2, 5, 6, 7, 8, 9, 10):
        loads[i].wait()

    live = keep[...].astype(F32) * rewards[...]
    end_row = ends[...].astype(F32)
    end_rows = jnp.broadcast_to(end_row, (8, SPAN)).astype(BF16)
    before = dot(end_rows, (row_i < col_i).astype(BF16))[0:1]
    end_total = before[:, SPAN - 1 : SPAN] + end_row[:, SPAN - 1 : SPAN]
    reach = ((row_i >= col_i) & (row_to_column(before, SPAN) == before)).astype(F32)
    local_sum = jnp.dot(
        jnp.broadcast_to(live, (8, SPAN)), reach, precision=FULL, preferred_element_type=F32
    )[0:1]
    open_row = (before == end_total).astype(F32)
    note[0:1, :] = jnp.broadcast_to(open_row[:, 0:1], (1, 128))
    note[1:2, :] = jnp.broadcast_to(local_sum[:, 0:1], (1, 128))
    note[2:8, :] = jnp.zeros((6, 128), F32)

    def tell(mask):
        return copy(note, box.at[mask], sn.at[mask], rn.at[mask], {"ctx": square_first + peer(mask)})

    def tell_back():
        return copy(later, got_later, sn.at[0], rn.at[0], {"ctx": lax.rem(me + last_square, count)})

    for mask in MASKS:
        tell(mask).start()

    scores[...] = lax.dot_general(c_in[...], b_in[...], (((1,), (1,)), ((), ())), preferred_element_type=F32)
    skip_cols = jnp.broadcast_to(skip[...], (8, 32))
    skip_parts = jnp.concatenate([*(one.astype(F32) for one in thirds(skip_cols)), jnp.zeros((8, 32), F32)], axis=1)
    for half in range(2):
        skip_lanes = dot(skip_parts.astype(BF16), pick(half))
        at = slice(512 * half, 512 * half + 512)
        base[:, at] = skip_lanes[0:1] * feat[:, at].astype(F32)
    causal = row_i[0:128, 0:128] >= col_i[0:128, 0:128]
    lane_head = lax.broadcasted_iota(jnp.int32, (SPAN, 128), 1) // HEAD_DIM

    def intra(unit):
        at = slice(unit * 128, unit * 128 + 128)
        aligned = unit // 2 * 8
        cum_rows = rows[aligned : 8 + aligned, :]
        step_rows = rows[32 + aligned : 40 + aligned, :]
        cum_cols = jnp.transpose(cum_rows)
        values = feat[:, at].astype(F32)
        top = base[0:128, at]
        low = base[128:256, at]
        for lane_h in range(4):
            h = lane_h + unit % 2 * 4
            masked = jnp.where(lane_head == lane_h, values, 0.0).astype(BF16)
            c_t0, c_t1 = cum_cols[0:128, h : h + 1], cum_cols[128:256, h : h + 1]
            c_s0, c_s1 = cum_rows[h : h + 1, 0:128], cum_rows[h : h + 1, 128:256]
            d_s0, d_s1 = step_rows[h : h + 1, 0:128], step_rows[h : h + 1, 128:256]
            w_tl = jnp.where(causal, scores[0:128, 0:128] * jnp.exp(c_t0 - c_s0) * d_s0, 0.0).astype(BF16)
            w_bl = (scores[128:256, 0:128] * jnp.exp(c_t1 - c_s0) * d_s0).astype(BF16)
            w_br = jnp.where(causal, scores[128:256, 128:256] * jnp.exp(c_t1 - c_s1) * d_s1, 0.0).astype(BF16)
            top = top + dot(w_tl, masked[0:128])
            low = low + dot(jnp.concatenate([w_bl, w_br], axis=1), masked)
        base[0:128, at] = top
        base[128:256, at] = low

    def rest():
        for unit in range(EARLY, GROUPS):
            intra(unit)

    for unit in range(EARLY):
        intra(unit)
    pl.when(square_first > 0)(rest)

    @pl.when(square_first < last_square)
    def _():
        pl.semaphore_wait(ready, 1)

    for i, (half, part) in enumerate(chunks):
        for mask in MASKS:
            gather_copy(mask, i).wait_recv()
        held = pl.ds(HEAD_ROWS + part * ROWS, ROWS)
        at = plain_rows(part)
        blocks = [square_state[k, half, held] for k in range(RANKS)]
        decays = [square_state[k, half, HEAD_ROWS - 1 : HEAD_ROWS] for k in range(RANKS)]

        @pl.when(square_first == 0)
        def _():
            second = blocks[0]
            third = decays[1] * second + blocks[1]
            fourth = decays[2] * third + blocks[2]
            passed[half, at] = decays[3] * fourth + blocks[3]
            pass_copy(i).start()
            enter[0, half, at] = jnp.zeros_like(second)
            enter[1, half, at] = second
            enter[2, half, at] = third
            enter[3, half, at] = fourth

        @pl.when(square_first > 0)
        def _():
            pass_copy(i).wait_recv()
            first = got_passed[half, at]
            second = decays[0] * first + blocks[0]
            third = decays[1] * second + blocks[1]
            fourth = decays[2] * third + blocks[2]

            @pl.when(square_first < last_square)
            def _():
                passed[half, at] = decays[3] * fourth + blocks[3]
                pass_copy(i).start()

            enter[0, half, at] = first
            enter[1, half, at] = second
            enter[2, half, at] = third
            enter[3, half, at] = fourth

        @pl.when(square_first > 0)
        def _():
            for mask in MASKS:
                enter_copy(mask, i).start()

    @pl.when(square_first == 0)
    def _():
        for i in range(len(chunks)):
            for mask in MASKS:
                enter_copy(mask, i).start()
        rest()

    for mask in MASKS:
        tell(mask).wait()
    box[0] = note[...]

    @pl.when(square_first == last_square)
    def _():
        got_later[...] = jnp.zeros((8, 128), F32)

    @pl.when(square_first < last_square)
    def _():
        tell_back().wait_recv()

    carry = got_later[1:2, :]
    whole = carry
    for k in range(RANKS - 1, -1, -1):
        link = box[jnp.bitwise_xor(rank, k)]
        whole = link[1:2] + link[0:1] * whole
        carry = jnp.where(k > rank, whole, carry)
    later[...] = jnp.broadcast_to(whole, (8, 128))

    @pl.when(square_first > 0)
    def _():
        tell_back().start()


    queries = c_in[...]
    readout = weight[...] * gain[...]
    sums[...] = jnp.zeros((8, SPAN), F32)
    for g in range(GROUPS):
        read_rows[g : g + 1, :] = readout[:, 128 * g : 128 * g + 128]

    def read(entering, group, held):
        square, linear = held
        hi, mid, _ = thirds(entering)
        carried = dot(queries, hi) + dot(queries, mid)
        at = pl.ds(pl.multiple_of(group * 128, 128), 128)
        mixed = base[:, at] + expl[:, at] * carried
        return square + mixed * mixed, linear + mixed * read_rows[pl.ds(group, 1), :]

    zero = jnp.zeros((SPAN, 128), F32)
    held = (zero, zero)
    for half in range(PARTS):
        held = read(enter[rank, half], rank + RANKS * half, held)
    for half in range(PARTS):
        for mask in MASKS:
            for i, (own_half, _) in enumerate(chunks):
                if own_half == half:
                    enter_copy(mask, i).wait_recv()
            held = read(got_enter[mask - 1, half], peer(mask) + RANKS * half, held)
    square, linear = held
    sums[0:1, :] = jnp.sum(jnp.transpose(square), axis=0, keepdims=True)
    sums[1:2, :] = jnp.sum(jnp.transpose(linear), axis=0, keepdims=True)
    head_copy = copy(sums, sums_other, sh, rh, {"head": other_head})
    head_copy.start()

    @pl.when(square_first > 0)
    def _():
        tell_back().wait_send()

    reward_total = local_sum + open_row * jnp.concatenate([carry, carry], axis=1)

    for i in range(len(chunks)):
        for mask in MASKS:
            gather_copy(mask, i).wait_send()
            enter_copy(mask, i).wait_send()

    @pl.when(square_first < last_square)
    def _():
        for i in range(len(chunks)):
            pass_copy(i).wait_send()

    head_copy.wait()
    both = sums[...] + sums_other[...]
    value = both[1:2] / jnp.sqrt(both[0:1] / (HEADS * HEAD_DIM) + NORM_EPSILON)
    out[0:1, :] = value
    out[1:2, :] = reward_total - value


def local(count, features, b_input, c_input, step_input, decay_log, skip_gain, norm_gain, value_weight, rewards, keep, ends):
    dma = pltpu.SemaphoreType.DMA
    pieces = PARTS * SPLIT
    quarter = (PARTS, 128, 128)
    operands = (
        features, b_input, c_input, step_input,
        decay_log.reshape(1, -1), skip_gain.reshape(1, -1), norm_gain.reshape(1, -1), value_weight.reshape(1, -1),
        rewards.reshape(1, -1), keep.reshape(1, -1), ends.reshape(1, -1),
    )
    result = pl.pallas_call(
        functools.partial(kernel, count),
        out_shape=jax.ShapeDtypeStruct((2, SPAN), F32),
        in_specs=[pl.BlockSpec(memory_space=pl.ANY)] * 11,
        out_specs=pl.BlockSpec(memory_space=pltpu.VMEM),
        scratch_shapes=[
            *[pltpu.VMEM(one.shape, one.dtype) for one in operands],
            dma((11,)),
            pltpu.VMEM((64, SPAN), F32),
            pltpu.VMEM((SPAN, 1024), F32),
            pltpu.VMEM((SPAN, 1024), F32),
            pltpu.VMEM((SPAN, SPAN), F32),
            pltpu.VMEM((GROUPS, HEAD_ROWS + 128, 128), F32),
            pltpu.VMEM((RANKS, PARTS, HEAD_ROWS + 128, 128), F32),
            pltpu.VMEM(quarter, F32),
            pltpu.VMEM(quarter, F32),
            pltpu.VMEM((RANKS, *quarter), F32),
            pltpu.VMEM((RANKS - 1, *quarter), F32),
            pltpu.VMEM((GROUPS, 128), F32),
            pltpu.VMEM((RANKS, 8, 128), F32),
            pltpu.VMEM((8, 128), F32),
            pltpu.VMEM((8, 128), F32),
            pltpu.VMEM((8, 128), F32),
            pltpu.VMEM((8, SPAN), F32),
            pltpu.VMEM((8, SPAN), F32),
            dma((RANKS - 1, pieces)), dma((RANKS - 1, pieces)),
            dma((pieces,)), dma((pieces,)),
            dma((RANKS - 1, pieces)), dma((RANKS - 1, pieces)),
            dma((RANKS,)), dma((RANKS,)),
            dma, dma,
            pltpu.SemaphoreType.REGULAR,
        ],
        compiler_params=pltpu.CompilerParams(
            collective_id=0, has_side_effects=True, vmem_limit_bytes=67043328
        ),
    )(*operands)
    return (result[0], result[1])


def solution(mesh):
    tokens = P(("traj", "ctx"))
    placed = (
        P(("traj", "ctx"), "head"),
        P(("traj", "ctx"), None),
        P(("traj", "ctx"), None),
        P("head", ("traj", "ctx")),
        P("head"), P("head"), P("head"), P("head"),
        tokens, tokens, tokens,
    )
    return jax.shard_map(
        functools.partial(local, mesh.shape["ctx"]),
        mesh=mesh,
        in_specs=placed,
        out_specs=(tokens, tokens),
        check_vma=False,
    )
```

```python
import functools

import jax
import jax.numpy as jnp
from jax import lax
from jax.experimental import pallas as pl
from jax.experimental.pallas import tpu as pltpu
from jax.sharding import PartitionSpec as P

HEADS = 64
HEAD_DIM = 32
SPAN = 256
NORM_EPSILON = 1e-05
FULL = lax.Precision.HIGHEST
MESH = pl.DeviceIdType.MESH
F32 = jnp.float32
BF16 = jnp.bfloat16
GROUPS = 8
RANKS = 4
PARTS = GROUPS // RANKS
SPLIT = 2
ROWS = 128 // SPLIT
HEAD_ROWS = 8
MASKS = (3, 1, 2)
EARLY = 5


def thirds(x):
    hi = x.astype(BF16)
    rest = x - hi.astype(F32)
    mid = rest.astype(BF16)
    lo = (rest - mid.astype(F32)).astype(BF16)
    return hi, mid, lo


def dot(a, b):
    return jnp.dot(a, b, preferred_element_type=F32)


def row_to_column(row, size):
    eye = lax.broadcasted_iota(jnp.int32, (size, size), 0) == lax.broadcasted_iota(jnp.int32, (size, size), 1)
    return jnp.sum(jnp.where(eye, jnp.broadcast_to(row, (size, size)), 0.0), axis=1, keepdims=True)


def kernel(
    count,
    *refs,
):
    sources, (out, *scratch) = refs[:11], refs[11:]
    here, sem_in = scratch[:11], scratch[11]
    run(count, sources, sem_in, out, *here, *scratch[12:])


def run(
    count, sources, sem_in, out,
    feat, b_in, c_in, step_in, decay_log, skip, gain, weight, rewards, keep, ends,
    rows, expl, base, scores, state, square_state, passed, got_passed, enter, got_enter, read_rows,
    box, note, later, got_later, sums, sums_other,
    s1, r1, s2, r2, s3, r3, sn, rn, sh, rh, ready,
):
    held_here = (feat, b_in, c_in, step_in, decay_log, skip, gain, weight, rewards, keep, ends)
    loads = [pltpu.make_async_copy(sources[i], held_here[i], sem_in.at[i]) for i in range(11)]
    for i in (3, 4, 0, 1, 2, 5, 6, 7, 8, 9, 10):
        loads[i].start()
    me = lax.axis_index("ctx")
    rank = lax.rem(me, RANKS)
    square_first = me - rank
    last_square = count - RANKS
    other_head = 1 - lax.axis_index("head")

    def peer(mask):
        return jnp.bitwise_xor(rank, mask)

    barrier = pltpu.get_barrier_semaphore()

    for mask in MASKS:
        pl.semaphore_signal(barrier, inc=1, device_id={"ctx": square_first + peer(mask)}, device_id_type=MESH)
    pl.semaphore_signal(barrier, inc=1, device_id={"head": other_head}, device_id_type=MESH)

    @pl.when(square_first < last_square)
    def _():
        pl.semaphore_signal(barrier, inc=1, device_id={"ctx": me + RANKS}, device_id_type=MESH)

    row_i = lax.broadcasted_iota(jnp.int32, (SPAN, SPAN), 0)
    col_i = lax.broadcasted_iota(jnp.int32, (SPAN, SPAN), 1)
    upto = (row_i <= col_i).astype(BF16)
    pick_row = lax.broadcasted_iota(jnp.int32, (128, 512), 0)
    pick_head = lax.broadcasted_iota(jnp.int32, (128, 512), 1) // HEAD_DIM
    pick_low = jnp.where(pick_row < 96, lax.rem(pick_row, 32), -1)

    def pick(half):
        return (pick_low == pick_head + 16 * half).astype(BF16)

    loads[3].wait()
    loads[4].wait()
    step = jax.nn.softplus(step_in[...])
    log_decay = -jnp.exp(row_to_column(decay_log[...], 32)) * step
    cum_parts = dot(jnp.concatenate(thirds(log_decay), axis=0), upto)
    cum = cum_parts[0:32] + cum_parts[32:64] + cum_parts[64:96]
    total = cum[:, SPAN - 1 : SPAN]
    rows[0:32, :] = cum
    rows[32:64, :] = step
    none = jnp.zeros((32, SPAN), BF16)

    def columns_of(values):
        stacked = jnp.concatenate([*thirds(values), none], axis=0)
        return jnp.transpose(stacked.astype(F32)).astype(BF16)

    scale_cols = columns_of(jnp.exp(total - cum) * step)
    grow_cols = columns_of(jnp.exp(cum))

    loads[0].wait()
    loads[1].wait()
    keys = jnp.transpose(b_in[...].astype(F32)).astype(BF16)

    def copy(src, dst, send, recv, where):
        return pltpu.make_async_remote_copy(
            src_ref=src, dst_ref=dst, send_sem=send, recv_sem=recv, device_id=where, device_id_type=MESH
        )

    def state_rows(part):
        first = HEAD_ROWS + part * ROWS
        return pl.ds(0, HEAD_ROWS + ROWS) if part == 0 else pl.ds(first, ROWS)

    def plain_rows(part):
        return pl.ds(part * ROWS, ROWS)

    chunks = [(half, part) for half in range(PARTS) for part in range(SPLIT)]

    def gather_copy(mask, i):
        half, part = chunks[i]
        at = state_rows(part)
        return copy(
            state.at[peer(mask) + RANKS * half, at], square_state.at[rank, half, at],
            s1.at[mask - 1, i], r1.at[mask - 1, i], {"ctx": square_first + peer(mask)},
        )

    def pass_copy(i):
        half, part = chunks[i]
        at = plain_rows(part)
        return copy(
            passed.at[half, at], got_passed.at[half, at], s2.at[i], r2.at[i], {"ctx": lax.rem(me + RANKS, count)}
        )

    def enter_copy(mask, i):
        half, part = chunks[i]
        at = plain_rows(part)
        return copy(
            enter.at[peer(mask), half, at], got_enter.at[mask - 1, half, at],
            s3.at[mask - 1, i], r3.at[mask - 1, i], {"ctx": square_first + peer(mask)},
        )

    def joined_copy(mask, half):
        return copy(
            enter.at[peer(mask), half], got_enter.at[mask - 1, half],
            s3.at[mask - 1, half * SPLIT], r3.at[mask - 1, half * SPLIT], {"ctx": square_first + peer(mask)},
        )

    for half in range(PARTS):
        at = slice(512 * half, 512 * half + 512)
        chosen = pick(half)
        scaled = (dot(scale_cols, chosen) * feat[:, at].astype(F32)).astype(BF16)
        block_state = dot(keys, scaled)
        decay = dot(grow_cols[SPAN - 16 : SPAN], chosen)[8:16]
        for g in range(RANKS):
            lanes = slice(128 * g, 128 * g + 128)
            state[RANKS * half + g, 0:HEAD_ROWS] = decay[:, lanes]
            state[RANKS * half + g, HEAD_ROWS : HEAD_ROWS + 128] = block_state[:, lanes]
        if half == 0:
            pl.semaphore_wait(barrier, RANKS + jnp.where(square_first > 0, 1, 0))

            @pl.when(square_first > 0)
            def _():
                pl.semaphore_signal(ready, inc=1, device_id={"ctx": me - RANKS}, device_id_type=MESH)
        for i, (own_half, _) in enumerate(chunks):
            if own_half == half:
                for mask in MASKS:
                    gather_copy(mask, i).start()
        square_state[rank, half] = state[rank + RANKS * half]

    for half in range(PARTS):
        expl[:, 512 * half : 512 * half + 512] = dot(grow_cols, pick(half))
    for i in (2, 5, 6, 7, 8, 9, 10):
        loads[i].wait()

    live = keep[...].astype(F32) * rewards[...]
    end_row = ends[...].astype(F32)
    end_rows = jnp.broadcast_to(end_row, (8, SPAN)).astype(BF16)
    before = dot(end_rows, (row_i < col_i).astype(BF16))[0:1]
    end_total = before[:, SPAN - 1 : SPAN] + end_row[:, SPAN - 1 : SPAN]
    reach = ((row_i >= col_i) & (row_to_column(before, SPAN) == before)).astype(F32)
    local_sum = jnp.dot(
        jnp.broadcast_to(live, (8, SPAN)), reach, precision=FULL, preferred_element_type=F32
    )[0:1]
    open_row = (before == end_total).astype(F32)
    note[0:1, :] = jnp.broadcast_to(open_row[:, 0:1], (1, 128))
    note[1:2, :] = jnp.broadcast_to(local_sum[:, 0:1], (1, 128))
    note[2:8, :] = jnp.zeros((6, 128), F32)

    def tell(mask):
        return copy(note, box.at[mask], sn.at[mask], rn.at[mask], {"ctx": square_first + peer(mask)})

    def tell_back():
        return copy(later, got_later, sn.at[0], rn.at[0], {"ctx": lax.rem(me + last_square, count)})

    for mask in MASKS:
        tell(mask).start()

    scores[...] = lax.dot_general(c_in[...], b_in[...], (((1,), (1,)), ((), ())), preferred_element_type=F32)
    skip_cols = jnp.broadcast_to(skip[...], (8, 32))
    skip_parts = jnp.concatenate([*(one.astype(F32) for one in thirds(skip_cols)), jnp.zeros((8, 32), F32)], axis=1)
    for half in range(2):
        skip_lanes = dot(skip_parts.astype(BF16), pick(half))
        at = slice(512 * half, 512 * half + 512)
        base[:, at] = skip_lanes[0:1] * feat[:, at].astype(F32)
    causal = row_i[0:128, 0:128] >= col_i[0:128, 0:128]
    lane_head = lax.broadcasted_iota(jnp.int32, (SPAN, 128), 1) // HEAD_DIM

    def intra(unit):
        at = slice(unit * 128, unit * 128 + 128)
        aligned = unit // 2 * 8
        cum_rows = rows[aligned : 8 + aligned, :]
        step_rows = rows[32 + aligned : 40 + aligned, :]
        cum_cols = jnp.transpose(cum_rows)
        values = feat[:, at].astype(F32)
        top = base[0:128, at]
        low = base[128:256, at]
        for lane_h in range(4):
            h = lane_h + unit % 2 * 4
            masked = jnp.where(lane_head == lane_h, values, 0.0).astype(BF16)
            c_t0, c_t1 = cum_cols[0:128, h : h + 1], cum_cols[128:256, h : h + 1]
            c_s0, c_s1 = cum_rows[h : h + 1, 0:128], cum_rows[h : h + 1, 128:256]
            d_s0, d_s1 = step_rows[h : h + 1, 0:128], step_rows[h : h + 1, 128:256]
            w_tl = jnp.where(causal, scores[0:128, 0:128] * jnp.exp(c_t0 - c_s0) * d_s0, 0.0).astype(BF16)
            w_bl = (scores[128:256, 0:128] * jnp.exp(c_t1 - c_s0) * d_s0).astype(BF16)
            w_br = jnp.where(causal, scores[128:256, 128:256] * jnp.exp(c_t1 - c_s1) * d_s1, 0.0).astype(BF16)
            top = top + dot(w_tl, masked[0:128])
            low = low + dot(jnp.concatenate([w_bl, w_br], axis=1), masked)
        base[0:128, at] = top
        base[128:256, at] = low

    def rest():
        for unit in range(EARLY, GROUPS):
            intra(unit)

    for unit in range(EARLY):
        intra(unit)
    pl.when(square_first > 0)(rest)

    @pl.when(square_first < last_square)
    def _():
        pl.semaphore_wait(ready, 1)

    for i, (half, part) in enumerate(chunks):
        for mask in MASKS:
            gather_copy(mask, i).wait_recv()
        held = pl.ds(HEAD_ROWS + part * ROWS, ROWS)
        at = plain_rows(part)
        blocks = [square_state[k, half, held] for k in range(RANKS)]
        decays = [square_state[k, half, HEAD_ROWS - 1 : HEAD_ROWS] for k in range(RANKS)]

        @pl.when(square_first == 0)
        def _():
            second = blocks[0]
            third = decays[1] * second + blocks[1]
            fourth = decays[2] * third + blocks[2]
            passed[half, at] = decays[3] * fourth + blocks[3]
            pass_copy(i).start()
            enter[0, half, at] = jnp.zeros_like(second)
            enter[1, half, at] = second
            enter[2, half, at] = third
            enter[3, half, at] = fourth

        @pl.when(square_first > 0)
        def _():
            pass_copy(i).wait_recv()
            first = got_passed[half, at]
            second = decays[0] * first + blocks[0]
            third = decays[1] * second + blocks[1]
            fourth = decays[2] * third + blocks[2]

            @pl.when(square_first < last_square)
            def _():
                passed[half, at] = decays[3] * fourth + blocks[3]
                pass_copy(i).start()

            enter[0, half, at] = first
            enter[1, half, at] = second
            enter[2, half, at] = third
            enter[3, half, at] = fourth

        @pl.when(square_first > 0)
        def _():
            for mask in MASKS:
                enter_copy(mask, i).start()

    @pl.when(square_first == 0)
    def _():
        for half in range(PARTS):
            for mask in (1, 3, 2):
                joined_copy(mask, half).start()
        rest()

    for mask in MASKS:
        tell(mask).wait()
    box[0] = note[...]

    @pl.when(square_first == last_square)
    def _():
        got_later[...] = jnp.zeros((8, 128), F32)

    @pl.when(square_first < last_square)
    def _():
        tell_back().wait_recv()

    carry = got_later[1:2, :]
    whole = carry
    for k in range(RANKS - 1, -1, -1):
        link = box[jnp.bitwise_xor(rank, k)]
        whole = link[1:2] + link[0:1] * whole
        carry = jnp.where(k > rank, whole, carry)
    later[...] = jnp.broadcast_to(whole, (8, 128))

    @pl.when(square_first > 0)
    def _():
        tell_back().start()


    queries = c_in[...]
    readout = weight[...] * gain[...]
    sums[...] = jnp.zeros((8, SPAN), F32)
    for g in range(GROUPS):
        read_rows[g : g + 1, :] = readout[:, 128 * g : 128 * g + 128]

    def read(entering, group, held):
        square, linear = held
        hi, mid, _ = thirds(entering)
        carried = dot(queries, hi) + dot(queries, mid)
        at = pl.ds(pl.multiple_of(group * 128, 128), 128)
        mixed = base[:, at] + expl[:, at] * carried
        return square + mixed * mixed, linear + mixed * read_rows[pl.ds(group, 1), :]

    zero = jnp.zeros((SPAN, 128), F32)
    held = (zero, zero)
    for half in range(PARTS):
        held = read(enter[rank, half], rank + RANKS * half, held)
    for half in range(PARTS):
        for mask in MASKS:

            @pl.when(square_first == 0)
            def _():
                joined_copy(mask, half).wait_recv()

            @pl.when(square_first > 0)
            def _():
                for i, (own_half, _) in enumerate(chunks):
                    if own_half == half:
                        enter_copy(mask, i).wait_recv()

            held = read(got_enter[mask - 1, half], peer(mask) + RANKS * half, held)
    square, linear = held
    sums[0:1, :] = jnp.sum(jnp.transpose(square), axis=0, keepdims=True)
    sums[1:2, :] = jnp.sum(jnp.transpose(linear), axis=0, keepdims=True)
    head_copy = copy(sums, sums_other, sh, rh, {"head": other_head})
    head_copy.start()

    @pl.when(square_first > 0)
    def _():
        tell_back().wait_send()

    reward_total = local_sum + open_row * jnp.concatenate([carry, carry], axis=1)

    for i in range(len(chunks)):
        for mask in MASKS:
            gather_copy(mask, i).wait_send()

    @pl.when(square_first == 0)
    def _():
        for half in range(PARTS):
            for mask in MASKS:
                joined_copy(mask, half).wait_send()

    @pl.when(square_first > 0)
    def _():
        for i in range(len(chunks)):
            for mask in MASKS:
                enter_copy(mask, i).wait_send()

    @pl.when(square_first < last_square)
    def _():
        for i in range(len(chunks)):
            pass_copy(i).wait_send()

    head_copy.wait()
    both = sums[...] + sums_other[...]
    value = both[1:2] / jnp.sqrt(both[0:1] / (HEADS * HEAD_DIM) + NORM_EPSILON)
    out[0:1, :] = value
    out[1:2, :] = reward_total - value


def local(count, features, b_input, c_input, step_input, decay_log, skip_gain, norm_gain, value_weight, rewards, keep, ends):
    dma = pltpu.SemaphoreType.DMA
    pieces = PARTS * SPLIT
    quarter = (PARTS, 128, 128)
    operands = (
        features, b_input, c_input, step_input,
        decay_log.reshape(1, -1), skip_gain.reshape(1, -1), norm_gain.reshape(1, -1), value_weight.reshape(1, -1),
        rewards.reshape(1, -1), keep.reshape(1, -1), ends.reshape(1, -1),
    )
    result = pl.pallas_call(
        functools.partial(kernel, count),
        out_shape=jax.ShapeDtypeStruct((2, SPAN), F32),
        in_specs=[pl.BlockSpec(memory_space=pl.ANY)] * 11,
        out_specs=pl.BlockSpec(memory_space=pltpu.VMEM),
        scratch_shapes=[
            *[pltpu.VMEM(one.shape, one.dtype) for one in operands],
            dma((11,)),
            pltpu.VMEM((64, SPAN), F32),
            pltpu.VMEM((SPAN, 1024), F32),
            pltpu.VMEM((SPAN, 1024), F32),
            pltpu.VMEM((SPAN, SPAN), F32),
            pltpu.VMEM((GROUPS, HEAD_ROWS + 128, 128), F32),
            pltpu.VMEM((RANKS, PARTS, HEAD_ROWS + 128, 128), F32),
            pltpu.VMEM(quarter, F32),
            pltpu.VMEM(quarter, F32),
            pltpu.VMEM((RANKS, *quarter), F32),
            pltpu.VMEM((RANKS - 1, *quarter), F32),
            pltpu.VMEM((GROUPS, 128), F32),
            pltpu.VMEM((RANKS, 8, 128), F32),
            pltpu.VMEM((8, 128), F32),
            pltpu.VMEM((8, 128), F32),
            pltpu.VMEM((8, 128), F32),
            pltpu.VMEM((8, SPAN), F32),
            pltpu.VMEM((8, SPAN), F32),
            dma((RANKS - 1, pieces)), dma((RANKS - 1, pieces)),
            dma((pieces,)), dma((pieces,)),
            dma((RANKS - 1, pieces)), dma((RANKS - 1, pieces)),
            dma((RANKS,)), dma((RANKS,)),
            dma, dma,
            pltpu.SemaphoreType.REGULAR,
        ],
        compiler_params=pltpu.CompilerParams(
            collective_id=0, has_side_effects=True, vmem_limit_bytes=67043328
        ),
    )(*operands)
    return (result[0], result[1])


def solution(mesh):
    tokens = P(("traj", "ctx"))
    placed = (
        P(("traj", "ctx"), "head"),
        P(("traj", "ctx"), None),
        P(("traj", "ctx"), None),
        P("head", ("traj", "ctx")),
        P("head"), P("head"), P("head"), P("head"),
        tokens, tokens, tokens,
    )
    return jax.shard_map(
        functools.partial(local, mesh.shape["ctx"]),
        mesh=mesh,
        in_specs=placed,
        out_specs=(tokens, tokens),
        check_vma=False,
    )
```
